256 devices in a mesh: dp: 32 (over y, x, core), mp: 8 (over z).
Axes of the slice: x: 4, y: 4, z: 8, core: 2. Of those that a mesh axis runs over, the one named last changes fastest.
Arguments:
- activations: bfloat16 [4096, 2560], P('dp'), may hold values from -6 to 6
- grad_hidden: bfloat16 [4096, 8192], P('dp', 'mp'), may hold values from -0.059814453 to 0.059814453
- up_weight: bfloat16 [2560, 8192], P('dp', 'mp'), may hold values from -6 to 6
- error_feedback: bfloat16 [32, 2560, 8192], P('dp', None, 'mp'), may hold values from -0.75 to 0.75
- query_previous: float32 [8192, 128], P('mp'), may hold values from -6 to 6
Outputs:
- grad_input: bfloat16 [4096, 2560], P('dp', 'mp')
- error_next: bfloat16 [32, 2560, 8192], P('dp', None, 'mp')
- update: float32 [2560, 8192], P('dp', 'mp')
- query_next: float32 [8192, 128], P('mp')
The draws below stay inside these ranges and needn't reach their ends.
All inputs are finite; a program needn't handle non-finite values.
Results may differ from the reference program's by a relative error of at most 0.0005.
Values may be sent and summed in bfloat16 or wider, within the bound.
No kernel may reach another device: no remote copies, remote signals or barrier semaphores. Data moves between devices by JAX's collectives and lax.ppermute only.
A program may use at most 128 MiB of HBM per device.

```python
import jax
import jax.numpy as jnp
from jax import lax

D = 2560
FF = 8192
R = 128
TOK_DEV = 128
TOKENS = 4096
N_DP = 32


def with_spikes(drawn, key, source, target, blocks, factor):
    def block_of(position):
        return (jnp.arange(drawn.shape[position]) // (drawn.shape[position] // blocks)).reshape((-1,) + (1,) * (drawn.ndim - 1 - position))

    near = jax.random.permutation(key, blocks)[block_of(target)]
    second = (block_of(target) + blocks // 2) % blocks
    return jnp.where((block_of(source) == near) | (block_of(source) == second), factor * drawn, drawn)


def level_of(rng, dims, split, smallest, largest):
    gain = 1.0
    for axis_at, blocks in split:
        draws = jax.random.uniform(jax.random.fold_in(jax.random.fold_in(rng, 6), axis_at), (blocks,), jnp.float32, smallest / len(split), largest / len(split))
        gain = gain * jnp.repeat(jnp.exp(draws), dims[axis_at] // blocks).reshape((-1,) + (1,) * (len(dims) - 1 - axis_at))
    return gain


def scatter_about(stream_key, extent, deviation, reach, split=(), kind=jnp.bfloat16):
    entries = jax.random.normal(stream_key, extent, jnp.float32) * deviation
    if len(split) > 0:
        entries = level_of(stream_key, extent, split, -0.22, 0.18) * entries
    return jnp.clip(entries, min=-reach, max=reach).astype(kind)


def noise_with(own_key, dims, scale, limit, shards, heavy, kind=jnp.bfloat16):
    result = scale * jax.random.normal(own_key, dims, jnp.float32)
    if shards:
        result = result * level_of(own_key, dims, shards, -0.22, 0.18)
    return jnp.clip(with_spikes(result, jax.random.fold_in(own_key, 3), *heavy), -limit, limit).astype(kind)


def setup_inputs(seed: int = 0) -> dict:
    arg_keys = jax.random.split(jax.random.key(seed), 6)
    return {
        "activations": noise_with(arg_keys[0], (TOKENS, D), 1.0, 6.0, ((0, 32),), (0, 1, 32, 2.75)),
        "grad_hidden": scatter_about(arg_keys[1], (TOKENS, FF), 0.01, 0.059814453, ((0, 32), (1, 8))),
        "up_weight": scatter_about(arg_keys[2], (D, FF), 1.0, 6.0, ((0, 32), (1, 8))),
        "error_feedback": scatter_about(arg_keys[3], (N_DP, D, FF), 0.125, 0.75, ((0, 32), (2, 8))),
        "query_previous": scatter_about(arg_keys[4], (FF, R), 1.0, 6.0, ((0, 8),), jnp.float32),
    }


HIGHEST = lax.Precision.HIGHEST

def merged_of(error_block, acts_block, hidden_block):
    return error_block.astype(jnp.float32) + jnp.dot(acts_block.T.astype(jnp.float32), hidden_block.astype(jnp.float32), preferred_element_type=jnp.float32)

def reference(activations, grad_hidden, up_weight, error_feedback, query_previous):
    grad_input = jnp.dot(grad_hidden.astype(jnp.float32), up_weight.T.astype(jnp.float32), preferred_element_type=jnp.float32).astype(jnp.bfloat16)
    acts_split = activations.reshape(N_DP, TOK_DEV, D)
    hidden_split = grad_hidden.reshape(N_DP, TOK_DEV, FF)
    stacked = (error_feedback, acts_split, hidden_split)

    def add_project(running, inputs):
        merged = merged_of(inputs[0], inputs[1], inputs[2])
        return (running + jnp.dot(merged.astype(jnp.float32), query_previous.astype(jnp.float32), precision=HIGHEST, preferred_element_type=jnp.float32), None)
    project, unused = lax.scan(add_project, jnp.zeros((D, R), jnp.float32), stacked)
    gram_matrix = jnp.dot(project.T.astype(jnp.float32), project.astype(jnp.float32), precision=HIGHEST, preferred_element_type=jnp.float32)
    factor = jnp.linalg.cholesky(gram_matrix)
    basis = lax.linalg.triangular_solve(factor, project, left_side=False, lower=True, transpose_a=True)

    def add_query(running, inputs):
        merged = merged_of(inputs[0], inputs[1], inputs[2])
        return (running + jnp.dot(merged.T.astype(jnp.float32), basis.astype(jnp.float32), precision=HIGHEST, preferred_element_type=jnp.float32), None)
    query_total, unused = lax.scan(add_query, jnp.zeros((FF, R), jnp.float32), stacked)
    query_next = query_total / N_DP
    update = jnp.dot(basis.astype(jnp.float32), query_next.T.astype(jnp.float32), precision=HIGHEST, preferred_element_type=jnp.float32)

    def residual_of(inputs):
        return (merged_of(inputs[0], inputs[1], inputs[2]) - update).astype(jnp.bfloat16)
    error_next = lax.map(residual_of, stacked)
    return (grad_input, error_next, update, query_next)
```

```python
import functools

import jax
import jax.numpy as jnp
from jax import lax
from jax.experimental import pallas as pl
from jax.experimental.pallas import tpu as pltpu
from jax.sharding import PartitionSpec as P

HIGHEST = lax.Precision.HIGHEST
F32 = jnp.float32
BF16 = jnp.bfloat16
BLOCK = 512
VMEM_LIMIT = 48 << 20


def dot(a, b, dims):
    return lax.dot_general(a, b, (dims, ((), ())), preferred_element_type=F32)


def pair(x):
    high = x.astype(BF16)
    rest = (x - high.astype(F32)).astype(BF16)
    return jnp.concatenate([high, rest], axis=1)


def folded(x):
    half = x.shape[1] // 2
    return x[:, :half] + x[:, half:]


def project_kernel(acts, hidden, error, query, out, query_pair, token_pair):
    @pl.when(pl.program_id(0) == 0)
    def _():
        split = pair(query[...])
        query_pair[...] = split
        token_pair[...] = pair(folded(dot(hidden[...], split, ((1,), (0,)))))

    total = dot(error[...], query_pair[...], ((1,), (0,)))
    total += dot(acts[...], token_pair[...], ((0,), (0,)))
    out[...] = folded(total)


def project_part(acts, hidden, error, query):
    tokens, rows = acts.shape
    columns, rank = query.shape
    return pl.pallas_call(
        project_kernel,
        grid=(rows // BLOCK,),
        in_specs=[
            pl.BlockSpec((tokens, BLOCK), lambda i: (0, i)),
            pl.BlockSpec((tokens, columns), lambda i: (0, 0)),
            pl.BlockSpec((BLOCK, columns), lambda i: (i, 0)),
            pl.BlockSpec((columns, rank), lambda i: (0, 0)),
        ],
        out_specs=pl.BlockSpec((BLOCK, rank), lambda i: (i, 0)),
        out_shape=jax.ShapeDtypeStruct((rows, rank), F32),
        scratch_shapes=[pltpu.VMEM((columns, 2 * rank), BF16), pltpu.VMEM((tokens, 2 * rank), BF16)],
        compiler_params=pltpu.CompilerParams(vmem_limit_bytes=VMEM_LIMIT),
        cost_estimate=pl.CostEstimate(
            flops=4 * rows * columns * rank, bytes_accessed=2 * rows * columns, transcendentals=0
        ),
        name="project_part",
    )(acts, hidden, error, query)


def query_kernel(acts, hidden, error, project, out, gram, total, tokens_sum, gram_sum):
    step = pl.program_id(0)

    @pl.when(step == 0)
    def _():
        total[...] = jnp.zeros_like(total)
        tokens_sum[...] = jnp.zeros_like(tokens_sum)
        gram_sum[...] = jnp.zeros_like(gram_sum)

    split = pair(project[...])
    total[...] += dot(error[...], split, ((0,), (0,)))
    tokens_sum[...] += dot(acts[...], split, ((1,), (0,)))
    gram_sum[...] += dot(split, split, ((0,), (0,)))

    @pl.when(step == pl.num_programs(0) - 1)
    def _():
        spread = pair(folded(tokens_sum[...]))
        out[...] = folded(total[...] + dot(hidden[...], spread, ((0,), (0,))))
        half = gram.shape[0]
        gram[...] = folded(gram_sum[:half, :] + gram_sum[half:, :])


def query_part(acts, hidden, error, project):
    tokens, rows = acts.shape
    columns = hidden.shape[1]
    rank = project.shape[1]
    return pl.pallas_call(
        query_kernel,
        grid=(rows // BLOCK,),
        in_specs=[
            pl.BlockSpec((tokens, BLOCK), lambda i: (0, i)),
            pl.BlockSpec((tokens, columns), lambda i: (0, 0)),
            pl.BlockSpec((BLOCK, columns), lambda i: (i, 0)),
            pl.BlockSpec((BLOCK, rank), lambda i: (i, 0)),
        ],
        out_specs=(
            pl.BlockSpec((columns, rank), lambda i: (0, 0)),
            pl.BlockSpec((rank, rank), lambda i: (0, 0)),
        ),
        out_shape=(
            jax.ShapeDtypeStruct((columns, rank), F32),
            jax.ShapeDtypeStruct((rank, rank), F32),
        ),
        scratch_shapes=[
            pltpu.VMEM((columns, 2 * rank), F32),
            pltpu.VMEM((tokens, 2 * rank), F32),
            pltpu.VMEM((2 * rank, 2 * rank), F32),
        ],
        compiler_params=pltpu.CompilerParams(vmem_limit_bytes=VMEM_LIMIT),
        cost_estimate=pl.CostEstimate(
            flops=4 * rows * columns * rank, bytes_accessed=2 * rows * columns, transcendentals=0
        ),
        name="query_part",
    )(acts, hidden, error, project)


def residual_kernel(acts, hidden, error, basis, basis_share, query, out, update, first, second):
    rank = query.shape[1]

    @pl.when(pl.program_id(0) == 0)
    def _():
        turned = query[...].T
        high = turned.astype(BF16)
        rest = (turned - high.astype(F32)).astype(BF16)
        first[:rank, :] = high
        first[rank:, :] = high
        second[:rank, :] = rest
        second[rank:, :] = -hidden[...]
        share = pair(basis_share[...])
        update[...] = dot(share, first[...], ((1,), (0,))) + dot(share[:, :rank], rest, ((1,), (0,)))

    split = pair(basis[...])
    mixed = jnp.concatenate([split[:, :rank], acts[...].T], axis=1)
    change = dot(split, first[...], ((1,), (0,))) + dot(mixed, second[...], ((1,), (0,)))
    out[...] = (error[...].astype(F32) - change).astype(BF16)


def residual(acts, hidden, error, basis, basis_share, query):
    tokens, rows = acts.shape
    columns, rank = query.shape
    share = basis_share.shape[0]
    return pl.pallas_call(
        residual_kernel,
        grid=(rows // BLOCK,),
        in_specs=[
            pl.BlockSpec((tokens, BLOCK), lambda i: (0, i)),
            pl.BlockSpec((tokens, columns), lambda i: (0, 0)),
            pl.BlockSpec((BLOCK, columns), lambda i: (i, 0)),
            pl.BlockSpec((BLOCK, rank), lambda i: (i, 0)),
            pl.BlockSpec((share, rank), lambda i: (0, 0)),
            pl.BlockSpec((columns, rank), lambda i: (0, 0)),
        ],
        out_specs=(
            pl.BlockSpec((BLOCK, columns), lambda i: (i, 0)),
            pl.BlockSpec((share, columns), lambda i: (0, 0)),
        ),
        out_shape=(
            jax.ShapeDtypeStruct((rows, columns), BF16),
            jax.ShapeDtypeStruct((share, columns), F32),
        ),
        scratch_shapes=[
            pltpu.VMEM((2 * rank, columns), BF16),
            pltpu.VMEM((rank + tokens, columns), BF16),
        ],
        compiler_params=pltpu.CompilerParams(vmem_limit_bytes=VMEM_LIMIT),
        cost_estimate=pl.CostEstimate(
            flops=8 * rows * columns * rank, bytes_accessed=4 * rows * columns, transcendentals=0
        ),
        name="residual",
    )(acts, hidden, error, basis, basis_share, query)


CORES = 2


def chips_of(replicas):
    return [list(range(core, replicas, CORES)) for core in range(CORES)]


def swapped(x, replicas):
    return lax.ppermute(x, "dp", [(i, i ^ 1) for i in range(replicas)])


def scatter_sum(x, replicas):
    core = lax.axis_index("dp") % CORES
    half = x.shape[0] // CORES
    theirs = swapped(lax.dynamic_slice_in_dim(x, (1 - core) * half, half, 0), replicas)
    x = lax.dynamic_slice_in_dim(x, core * half, half, 0) + theirs
    chips = replicas // CORES
    pieces = lax.all_to_all(
        x.reshape(chips, half // chips, -1), "dp", 0, 0, axis_index_groups=chips_of(replicas)
    )
    return jnp.sum(pieces, axis=0)


def gather_rows(x, replicas):
    chips = replicas // CORES
    spread = jnp.broadcast_to(x[None], (chips, *x.shape))
    mine = lax.all_to_all(spread, "dp", 0, 0, axis_index_groups=chips_of(replicas))
    mine = mine.reshape(chips * x.shape[0], -1)
    theirs = swapped(mine, replicas)
    core = lax.axis_index("dp") % CORES
    return jnp.where(
        core == 0, jnp.concatenate([mine, theirs], 0), jnp.concatenate([theirs, mine], 0)
    )


def sum_over_mp(x):
    ranks = lax.axis_size("mp")
    spread = jnp.broadcast_to(x[None], (ranks, *x.shape))
    return jnp.sum(lax.all_to_all(spread, "mp", 0, 0), axis=0)


def inverse_factor(gram_matrix):
    factor = jnp.linalg.cholesky(gram_matrix)
    identity = jnp.eye(gram_matrix.shape[0], dtype=F32)
    return lax.linalg.triangular_solve(factor, identity, left_side=False, lower=True, transpose_a=True)


def local(activations, grad_hidden, up_weight, error_feedback, query_previous):
    replicas = lax.axis_size("dp")
    error = error_feedback[0]
    partial_input = lax.dot_general(
        grad_hidden,
        lax.all_gather(up_weight, "dp", axis=0, tiled=True),
        (((1,), (1,)), ((), ())),
        preferred_element_type=F32,
    )
    grad_input = lax.psum_scatter(partial_input, "mp", scatter_dimension=1, tiled=True).astype(BF16)

    part = project_part(activations, grad_hidden, error, query_previous)
    project = gather_rows(sum_over_mp(scatter_sum(part, replicas)), replicas)
    part, gram_matrix = query_part(activations, grad_hidden, error, project)
    inverse = inverse_factor(gram_matrix)
    total = gather_rows(scatter_sum(part, replicas), replicas)
    basis = jnp.dot(project, inverse, precision=HIGHEST, preferred_element_type=F32)
    query_next = jnp.dot(total, inverse, precision=HIGHEST, preferred_element_type=F32) / replicas
    share = basis.shape[0] // replicas
    basis_share = lax.dynamic_slice_in_dim(basis, lax.axis_index("dp") * share, share, 0)
    error_next, update = residual(
        activations, grad_hidden, error, basis, basis_share, query_next
    )
    return (grad_input, error_next[None], update, query_next)


def solution(mesh):
    in_specs = (P("dp", None), P("dp", "mp"), P("dp", "mp"), P("dp", None, "mp"), P("mp", None))
    out_specs = (P("dp", "mp"), P("dp", None, "mp"), P("dp", "mp"), P("mp", None))
    return jax.shard_map(local, mesh=mesh, in_specs=in_specs, out_specs=out_specs, check_vma=False)
```

```python
import functools

import jax
import jax.numpy as jnp
from jax import lax
from jax.experimental import pallas as pl
from jax.experimental.pallas import tpu as pltpu
from jax.sharding import PartitionSpec as P

HIGHEST = lax.Precision.HIGHEST
F32 = jnp.float32
BF16 = jnp.bfloat16
BLOCK = 512
VMEM_LIMIT = 48 << 20


def dot(a, b, dims):
    return lax.dot_general(a, b, (dims, ((), ())), preferred_element_type=F32)


def pair(x):
    high = x.astype(BF16)
    rest = (x - high.astype(F32)).astype(BF16)
    return jnp.concatenate([high, rest], axis=1)


def folded(x):
    half = x.shape[1] // 2
    return x[:, :half] + x[:, half:]


def project_kernel(acts, hidden, error, query, out, query_pair, token_pair):
    @pl.when(pl.program_id(0) == 0)
    def _():
        split = pair(query[...])
        query_pair[...] = split
        token_pair[...] = pair(folded(dot(hidden[...], split, ((1,), (0,)))))

    total = dot(error[...], query_pair[...], ((1,), (0,)))
    total += dot(acts[...], token_pair[...], ((0,), (0,)))
    out[...] = folded(total)


def project_part(acts, hidden, error, query):
    tokens, rows = acts.shape
    columns, rank = query.shape
    return pl.pallas_call(
        project_kernel,
        grid=(rows // BLOCK,),
        in_specs=[
            pl.BlockSpec((tokens, BLOCK), lambda i: (0, i)),
            pl.BlockSpec((tokens, columns), lambda i: (0, 0)),
            pl.BlockSpec((BLOCK, columns), lambda i: (i, 0)),
            pl.BlockSpec((columns, rank), lambda i: (0, 0)),
        ],
        out_specs=pl.BlockSpec((BLOCK, rank), lambda i: (i, 0)),
        out_shape=jax.ShapeDtypeStruct((rows, rank), F32),
        scratch_shapes=[pltpu.VMEM((columns, 2 * rank), BF16), pltpu.VMEM((tokens, 2 * rank), BF16)],
        compiler_params=pltpu.CompilerParams(vmem_limit_bytes=VMEM_LIMIT),
        cost_estimate=pl.CostEstimate(
            flops=4 * rows * columns * rank, bytes_accessed=2 * rows * columns, transcendentals=0
        ),
        name="project_part",
    )(acts, hidden, error, query)


def query_kernel(acts, hidden, error, project, out, gram, total, tokens_sum, gram_sum):
    step = pl.program_id(0)

    @pl.when(step == 0)
    def _():
        total[...] = jnp.zeros_like(total)
        tokens_sum[...] = jnp.zeros_like(tokens_sum)
        gram_sum[...] = jnp.zeros_like(gram_sum)

    split = pair(project[...])
    total[...] += dot(error[...], split, ((0,), (0,)))
    tokens_sum[...] += dot(acts[...], split, ((1,), (0,)))
    gram_sum[...] += dot(split, split, ((0,), (0,)))

    @pl.when(step == pl.num_programs(0) - 1)
    def _():
        spread = pair(folded(tokens_sum[...]))
        out[...] = folded(total[...] + dot(hidden[...], spread, ((0,), (0,))))
        half = gram.shape[0]
        gram[...] = folded(gram_sum[:half, :] + gram_sum[half:, :])


def query_part(acts, hidden, error, project):
    tokens, rows = acts.shape
    columns = hidden.shape[1]
    rank = project.shape[1]
    return pl.pallas_call(
        query_kernel,
        grid=(rows // BLOCK,),
        in_specs=[
            pl.BlockSpec((tokens, BLOCK), lambda i: (0, i)),
            pl.BlockSpec((tokens, columns), lambda i: (0, 0)),
            pl.BlockSpec((BLOCK, columns), lambda i: (i, 0)),
            pl.BlockSpec((BLOCK, rank), lambda i: (i, 0)),
        ],
        out_specs=(
            pl.BlockSpec((columns, rank), lambda i: (0, 0)),
            pl.BlockSpec((rank, rank), lambda i: (0, 0)),
        ),
        out_shape=(
            jax.ShapeDtypeStruct((columns, rank), F32),
            jax.ShapeDtypeStruct((rank, rank), F32),
        ),
        scratch_shapes=[
            pltpu.VMEM((columns, 2 * rank), F32),
            pltpu.VMEM((tokens, 2 * rank), F32),
            pltpu.VMEM((2 * rank, 2 * rank), F32),
        ],
        compiler_params=pltpu.CompilerParams(vmem_limit_bytes=VMEM_LIMIT),
        cost_estimate=pl.CostEstimate(
            flops=4 * rows * columns * rank, bytes_accessed=2 * rows * columns, transcendentals=0
        ),
        name="query_part",
    )(acts, hidden, error, project)


def residual_kernel(acts, hidden, error, basis, basis_share, query, out, update, factors):
    rank = query.shape[1]

    @pl.when(pl.program_id(0) == 0)
    def _():
        turned = query[...].T
        high = turned.astype(BF16)
        rest = (turned - high.astype(F32)).astype(BF16)
        factors[:rank, :] = high
        factors[rank : 2 * rank, :] = high
        factors[2 * rank : 3 * rank, :] = rest
        factors[3 * rank :, :] = -hidden[...]
        share = pair(basis_share[...])
        share = jnp.concatenate([share, share[:, :rank]], axis=1)
        update[...] = dot(share, factors[: 3 * rank, :], ((1,), (0,)))

    split = pair(basis[...])
    mixed = jnp.concatenate([split, split[:, :rank], acts[...].T], axis=1)
    change = dot(mixed, factors[...], ((1,), (0,)))
    out[...] = (error[...].astype(F32) - change).astype(BF16)


def residual(acts, hidden, error, basis, basis_share, query):
    tokens, rows = acts.shape
    columns, rank = query.shape
    share = basis_share.shape[0]
    return pl.pallas_call(
        residual_kernel,
        grid=(rows // BLOCK,),
        in_specs=[
            pl.BlockSpec((tokens, BLOCK), lambda i: (0, i)),
            pl.BlockSpec((tokens, columns), lambda i: (0, 0)),
            pl.BlockSpec((BLOCK, columns), lambda i: (i, 0)),
            pl.BlockSpec((BLOCK, rank), lambda i: (i, 0)),
            pl.BlockSpec((share, rank), lambda i: (0, 0)),
            pl.BlockSpec((columns, rank), lambda i: (0, 0)),
        ],
        out_specs=(
            pl.BlockSpec((BLOCK, columns), lambda i: (i, 0)),
            pl.BlockSpec((share, columns), lambda i: (0, 0)),
        ),
        out_shape=(
            jax.ShapeDtypeStruct((rows, columns), BF16),
            jax.ShapeDtypeStruct((share, columns), F32),
        ),
        scratch_shapes=[
            pltpu.VMEM((3 * rank + tokens, columns), BF16),
        ],
        compiler_params=pltpu.CompilerParams(vmem_limit_bytes=VMEM_LIMIT),
        cost_estimate=pl.CostEstimate(
            flops=8 * rows * columns * rank, bytes_accessed=4 * rows * columns, transcendentals=0
        ),
        name="residual",
    )(acts, hidden, error, basis, basis_share, query)


CORES = 2


def chips_of(replicas):
    return [list(range(core, replicas, CORES)) for core in range(CORES)]


def swapped(x, replicas):
    return lax.ppermute(x, "dp", [(i, i ^ 1) for i in range(replicas)])


def scatter_sum(x, replicas):
    core = lax.axis_index("dp") % CORES
    half = x.shape[0] // CORES
    theirs = swapped(lax.dynamic_slice_in_dim(x, (1 - core) * half, half, 0), replicas)
    x = lax.dynamic_slice_in_dim(x, core * half, half, 0) + theirs
    chips = replicas // CORES
    pieces = lax.all_to_all(
        x.reshape(chips, half // chips, -1), "dp", 0, 0, axis_index_groups=chips_of(replicas)
    )
    return jnp.sum(pieces, axis=0)


def gather_rows(x, replicas):
    chips = replicas // CORES
    spread = jnp.broadcast_to(x[None], (chips, *x.shape))
    mine = lax.all_to_all(spread, "dp", 0, 0, axis_index_groups=chips_of(replicas))
    mine = mine.reshape(chips * x.shape[0], -1)
    theirs = swapped(mine, replicas)
    core = lax.axis_index("dp") % CORES
    return jnp.where(
        core == 0, jnp.concatenate([mine, theirs], 0), jnp.concatenate([theirs, mine], 0)
    )


def sum_over_mp(x):
    ranks = lax.axis_size("mp")
    spread = jnp.broadcast_to(x[None], (ranks, *x.shape))
    return jnp.sum(lax.all_to_all(spread, "mp", 0, 0), axis=0)


SUB = 8


def inverse_factor_kernel(gram, out, table):
    rank = gram.shape[0]
    table[:, :rank] = gram[...]
    row = lax.broadcasted_iota(jnp.int32, (rank, rank), 0)
    column = lax.broadcasted_iota(jnp.int32, (rank, rank), 1)
    table[:, rank:] = jnp.where(row == column, 1.0, 0.0)
    place = lax.broadcasted_iota(jnp.int32, (SUB, 2 * rank), 0)
    for first in range(0, rank, SUB):
        panel = table[first : first + SUB, :]
        for j in range(SUB):
            across = panel[:, first + j : first + j + 1]
            pivot = across[j : j + 1, :]
            scale = lax.rsqrt(pivot)
            scale = scale * (1.5 - 0.5 * pivot * scale * scale)
            solved = panel[j : j + 1, :] * scale
            reduced = panel - (across * scale) * solved
            panel = jnp.where(place > j, reduced, jnp.where(place == j, solved, panel))
        table[first : first + SUB, :] = panel
        if first + SUB < rank:
            change = lax.dot_general(
                panel[:, :rank],
                panel,
                (((0,), (0,)), ((), ())),
                precision=HIGHEST,
                preferred_element_type=F32,
            )
            table[first + SUB :, :] -= change[first + SUB :, :]
    out[...] = table[:, rank:].T


def inverse_factor(gram_matrix):
    rank = gram_matrix.shape[0]
    return pl.pallas_call(
        inverse_factor_kernel,
        out_shape=jax.ShapeDtypeStruct((rank, rank), F32),
        grid=(1,),
        in_specs=[pl.BlockSpec((rank, rank), lambda i: (0, 0))],
        out_specs=pl.BlockSpec((rank, rank), lambda i: (0, 0)),
        scratch_shapes=[pltpu.VMEM((rank, 2 * rank), F32)],
        compiler_params=pltpu.CompilerParams(vmem_limit_bytes=VMEM_LIMIT),
        cost_estimate=pl.CostEstimate(flops=2 * 10**9, bytes_accessed=10**7, transcendentals=128),
        name="inverse_factor",
    )(gram_matrix)


def input_gradient(grad_hidden, up_weight, replicas):
    core = lax.axis_index("dp") % CORES
    theirs = swapped(grad_hidden, replicas)
    both = jnp.concatenate(
        [jnp.where(core == 0, grad_hidden, theirs), jnp.where(core == 0, theirs, grad_hidden)], 0
    )
    weight = lax.all_gather(
        up_weight, "dp", axis=0, tiled=True, axis_index_groups=chips_of(replicas)
    )
    partial_input = dot(both, weight, ((1,), (1,)))
    turned = lax.psum_scatter(partial_input, "mp", scatter_dimension=1, tiled=True).astype(BF16).T
    tokens, share = grad_hidden.shape[0], up_weight.shape[0]
    mine = jnp.where(core == 0, turned[:, :tokens], turned[:, tokens:])
    other = swapped(jnp.where(core == 0, turned[:, tokens:], turned[:, :tokens]), replicas)
    mine, other = (x.reshape(-1, 1, share, tokens) for x in (mine, other))
    ordered = jnp.where(
        core == 0, jnp.concatenate([mine, other], 1), jnp.concatenate([other, mine], 1)
    )
    return ordered.reshape(-1, tokens).T


def local(activations, grad_hidden, up_weight, error_feedback, query_previous):
    replicas = lax.axis_size("dp")
    error = error_feedback[0]
    grad_input = input_gradient(grad_hidden, up_weight, replicas)

    part = project_part(activations, grad_hidden, error, query_previous)
    project = gather_rows(sum_over_mp(scatter_sum(part, replicas)), replicas)
    part, gram_matrix = query_part(activations, grad_hidden, error, project)
    inverse = inverse_factor(gram_matrix)
    total = gather_rows(scatter_sum(part, replicas), replicas)
    basis = jnp.dot(project, inverse, precision=HIGHEST, preferred_element_type=F32)
    query_next = jnp.dot(total, inverse, precision=HIGHEST, preferred_element_type=F32) / replicas
    share = basis.shape[0] // replicas
    basis_share = lax.dynamic_slice_in_dim(basis, lax.axis_index("dp") * share, share, 0)
    error_next, update = residual(
        activations, grad_hidden, error, basis, basis_share, query_next
    )
    return (grad_input, error_next[None], update, query_next)


def solution(mesh):
    in_specs = (P("dp", None), P("dp", "mp"), P("dp", "mp"), P("dp", None, "mp"), P("mp", None))
    out_specs = (P("dp", "mp"), P("dp", None, "mp"), P("dp", "mp"), P("mp", None))
    return jax.shard_map(local, mesh=mesh, in_specs=in_specs, out_specs=out_specs, check_vma=False)
```

```python
import functools

import jax
import jax.numpy as jnp
from jax import lax
from jax.experimental import pallas as pl
from jax.experimental.pallas import tpu as pltpu
from jax.sharding import PartitionSpec as P

HIGHEST = lax.Precision.HIGHEST
F32 = jnp.float32
BF16 = jnp.bfloat16
BLOCK = 640
CORES = 2
VMEM_LIMIT = 48 << 20

def dot(a, b, dims):
    return lax.dot_general(a, b, (dims, ((), ())), preferred_element_type=F32)

def pair(x):
    high = x.astype(BF16)
    rest = (x - high.astype(F32)).astype(BF16)
    return jnp.concatenate([high, rest], axis=1)

def folded(x):
    half = x.shape[1] // 2
    return x[:, :half] + x[:, half:]

def load(source, target, sem):
    copy = pltpu.make_async_copy(source, target, sem)
    copy.start()
    return copy

def row_of(step, core, rows):
    half = rows // CORES
    steps = half // BLOCK
    own = jnp.where(step < steps, core, 1 - core)
    return pl.multiple_of(own * half + lax.rem(step, steps) * BLOCK, BLOCK)

def start_rows(core, error, error_rows, sems):
    rows = error.shape[0]

    def start(step, carry):
        load(error.at[pl.ds(row_of(step, core, rows), BLOCK)], error_rows.at[step], sems.at[step])
        return carry

    lax.fori_loop(0, rows // BLOCK, start, 0)

def wait_rows(step, error, error_rows, sems):
    pltpu.make_async_copy(error.at[pl.ds(0, BLOCK)], error_rows.at[step], sems.at[step]).wait()

def halves(core, rows, body, first, second):
    steps = rows // CORES // BLOCK
    for base, ref in ((0, first), (steps, second)):

        def step_of(i, carry, base=base, ref=ref):
            body(base + i, row_of(base + i, core, rows), pl.multiple_of(i * BLOCK, BLOCK), ref)
            return carry

        lax.fori_loop(0, steps, step_of, 0)

def project_kernel(place, acts, hidden, error, query, mine, theirs,
                   acts_in, hidden_in, query_in, error_rows, query_pair, token_pair, small, sems):
    core = place[0]
    copies = [
        load(query, query_in, small.at[0]),
        load(hidden, hidden_in, small.at[1]),
        load(acts, acts_in, small.at[2]),
    ]
    start_rows(core, error, error_rows, sems)
    copies[0].wait()
    split = pair(query_in[...])
    query_pair[...] = split
    copies[1].wait()
    token_pair[...] = pair(folded(dot(hidden_in[...], split, ((1,), (0,)))))
    copies[2].wait()

    def body(step, row, at, ref):
        wait_rows(step, error, error_rows, sems)
        total = dot(error_rows[step], query_pair[...], ((1,), (0,)))
        total += dot(acts_in[:, pl.ds(row, BLOCK)], token_pair[...], ((0,), (0,)))
        ref[pl.ds(at, BLOCK), :] = folded(total)

    halves(core, error.shape[0], body, mine, theirs)

HBM = pl.BlockSpec(memory_space=pltpu.HBM)
SCALARS = pl.BlockSpec(memory_space=pltpu.SMEM)

def whole(shape):
    return pl.BlockSpec(shape, lambda i: (0,) * len(shape))

def project_part(place, acts, hidden, error, query):
    tokens, rows = acts.shape
    columns, rank = query.shape
    half = (rows // CORES, rank)
    return pl.pallas_call(
        project_kernel,
        grid=(1,),
        in_specs=[SCALARS, HBM, HBM, HBM, HBM],
        out_specs=(whole(half), whole(half)),
        out_shape=(jax.ShapeDtypeStruct(half, F32),) * 2,
        scratch_shapes=[
            pltpu.VMEM((tokens, rows), BF16),
            pltpu.VMEM((tokens, columns), BF16),
            pltpu.VMEM((columns, rank), F32),
            pltpu.VMEM((rows // BLOCK, BLOCK, columns), BF16),
            pltpu.VMEM((columns, 2 * rank), BF16),
            pltpu.VMEM((tokens, 2 * rank), BF16),
            pltpu.SemaphoreType.DMA((3,)),
            pltpu.SemaphoreType.DMA((rows // BLOCK,)),
        ],
        compiler_params=pltpu.CompilerParams(vmem_limit_bytes=60 << 20),
        cost_estimate=pl.CostEstimate(
            flops=4 * rows * columns * rank, bytes_accessed=2 * rows * columns, transcendentals=0
        ),
        name="project_part",
    )(place, acts, hidden, error, query)

def query_kernel(place, acts, hidden, error, own, other, mine, theirs, gram,
                 acts_in, hidden_in, error_rows, total, tokens_sum, gram_sum, small, sems):
    core = place[0]
    rank = gram.shape[0]
    acts_copy = load(acts, acts_in, small.at[0])
    start_rows(core, error, error_rows, sems)
    hidden_copy = load(hidden, hidden_in, small.at[1])
    total[...] = jnp.zeros_like(total)
    tokens_sum[...] = jnp.zeros_like(tokens_sum)
    gram_sum[...] = jnp.zeros_like(gram_sum)
    acts_copy.wait()

    def body(step, row, at, ref):
        split = pair(ref[pl.ds(at, BLOCK), :])
        gram_sum[...] += dot(split, split, ((0,), (0,)))
        tokens_sum[...] += dot(acts_in[:, pl.ds(row, BLOCK)], split, ((1,), (0,)))
        wait_rows(step, error, error_rows, sems)
        total[...] += dot(split, error_rows[step], ((0,), (0,)))

    halves(core, error.shape[0], body, own, other)
    hidden_copy.wait()
    spread = pair(folded(tokens_sum[...]))
    turned = total[...] + dot(spread, hidden_in[...], ((0,), (0,)))
    total[:rank, :] = turned[:rank, :] + turned[rank:, :]
    half = mine.shape[0]
    mine[...] = total[:rank, pl.ds(pl.multiple_of(core * half, half), half)].T
    theirs[...] = total[:rank, pl.ds(pl.multiple_of((1 - core) * half, half), half)].T
    gram[...] = folded(gram_sum[:rank, :] + gram_sum[rank:, :])

def query_part(place, acts, hidden, error, own, other):
    tokens, rows = acts.shape
    columns = hidden.shape[1]
    rank = own.shape[1]
    half = (columns // CORES, rank)
    return pl.pallas_call(
        query_kernel,
        grid=(1,),
        in_specs=[SCALARS, HBM, HBM, HBM, whole(own.shape), whole(own.shape)],
        out_specs=(whole(half), whole(half), whole((rank, rank))),
        out_shape=(
            jax.ShapeDtypeStruct(half, F32),
            jax.ShapeDtypeStruct(half, F32),
            jax.ShapeDtypeStruct((rank, rank), F32),
        ),
        scratch_shapes=[
            pltpu.VMEM((tokens, rows), BF16),
            pltpu.VMEM((tokens, columns), BF16),
            pltpu.VMEM((rows // BLOCK, BLOCK, columns), BF16),
            pltpu.VMEM((2 * rank, columns), F32),
            pltpu.VMEM((tokens, 2 * rank), F32),
            pltpu.VMEM((2 * rank, 2 * rank), F32),
            pltpu.SemaphoreType.DMA((2,)),
            pltpu.SemaphoreType.DMA((rows // BLOCK,)),
        ],
        compiler_params=pltpu.CompilerParams(vmem_limit_bytes=VMEM_LIMIT),
        cost_estimate=pl.CostEstimate(
            flops=4 * rows * columns * rank, bytes_accessed=2 * rows * columns, transcendentals=0
        ),
        name="query_part",
    )(place, acts, hidden, error, own, other)

def triple(x):
    split = pair(x)
    return jnp.concatenate([split, split[:, : x.shape[1]]], axis=1)

def stacked(x):
    high = x.astype(BF16)
    rest = (x - high.astype(F32)).astype(BF16)
    return jnp.concatenate([high, high, rest], axis=0)

def residual_kernel(place, acts, hidden, error, own, other, inverse, query_own, query_other,
                    out, update, query,
                    acts_in, hidden_in, error_rows, turn, factors, small, sems, sent):
    core, replica, replicas = place[0], place[1], place[2]
    rank = inverse.shape[0]
    rows = error.shape[0]
    acts_copy = load(acts, acts_in, small.at[0])
    hidden_copy = load(hidden, hidden_in, small.at[1])
    start_rows(core, error, error_rows, sems)
    turn[...] = stacked(inverse[...])
    scale = 1.0 / replicas.astype(F32)
    half = query_own.shape[0]
    for ref, first in ((query_own, core * half), (query_other, (1 - core) * half)):
        query[pl.ds(pl.multiple_of(first, half), half), :] = (
            dot(triple(ref[...]), turn[...], ((1,), (0,))) * scale
        )
    factors[: 3 * rank, :] = stacked(query[...].T)
    hidden_copy.wait()
    factors[3 * rank :, :] = -hidden_in[...]
    share = update.shape[0]
    first = replica * share
    within = lax.rem(first, rows // CORES)
    at = pl.ds(pl.multiple_of(within, 8), share)
    own_half = jnp.where(first < rows // CORES, 0, 1) == core
    picked = jnp.where(own_half, own[at, :], other[at, :])
    basis = dot(triple(picked), turn[...], ((1,), (0,)))
    update[...] = dot(triple(basis), factors[: 3 * rank, :], ((1,), (0,)))
    acts_copy.wait()

    def body(step, row, at, ref):
        basis = dot(triple(ref[pl.ds(at, BLOCK), :]), turn[...], ((1,), (0,)))
        mixed = jnp.concatenate([triple(basis), acts_in[:, pl.ds(row, BLOCK)].T], axis=1)
        change = dot(mixed, factors[...], ((1,), (0,)))
        wait_rows(step, error, error_rows, sems)
        error_rows[step] = (error_rows[step].astype(F32) - change).astype(BF16)
        load(error_rows.at[step], out.at[pl.ds(row, BLOCK)], sent.at[step])

    halves(core, rows, body, own, other)

    def drain(step, carry):
        pltpu.make_async_copy(error_rows.at[step], out.at[pl.ds(0, BLOCK)], sent.at[step]).wait()
        return carry

    lax.fori_loop(0, rows // BLOCK, drain, 0)

def residual(place, acts, hidden, error, own, other, inverse, query_own, query_other, share):
    tokens, rows = acts.shape
    columns = hidden.shape[1]
    rank = inverse.shape[0]
    return pl.pallas_call(
        residual_kernel,
        grid=(1,),
        in_specs=[
            SCALARS, HBM, HBM, HBM, whole(own.shape), whole(own.shape), whole(inverse.shape),
            whole(query_own.shape), whole(query_own.shape),
        ],
        out_specs=(HBM, whole((share, columns)), whole((columns, rank))),
        out_shape=(
            jax.ShapeDtypeStruct((rows, columns), BF16),
            jax.ShapeDtypeStruct((share, columns), F32),
            jax.ShapeDtypeStruct((columns, rank), F32),
        ),
        scratch_shapes=[
            pltpu.VMEM((tokens, rows), BF16),
            pltpu.VMEM((tokens, columns), BF16),
            pltpu.VMEM((rows // BLOCK, BLOCK, columns), BF16),
            pltpu.VMEM((3 * rank, rank), BF16),
            pltpu.VMEM((3 * rank + tokens, columns), BF16),
            pltpu.SemaphoreType.DMA((2,)),
            pltpu.SemaphoreType.DMA((rows // BLOCK,)),
            pltpu.SemaphoreType.DMA((rows // BLOCK,)),
        ],
        compiler_params=pltpu.CompilerParams(vmem_limit_bytes=VMEM_LIMIT),
        cost_estimate=pl.CostEstimate(
            flops=8 * rows * columns * rank, bytes_accessed=4 * rows * columns, transcendentals=0
        ),
        name="residual",
    )(place, acts, hidden, error, own, other, inverse, query_own, query_other)


def chips_of(replicas):
    return [list(range(core, replicas, CORES)) for core in range(CORES)]

def swapped(x, replicas):
    return lax.ppermute(x, "dp", [(i, i ^ 1) for i in range(replicas)])

def scatter_sum(mine, theirs, replicas):
    x = mine + swapped(theirs, replicas)
    chips = replicas // CORES
    pieces = lax.all_to_all(
        x.reshape(chips, x.shape[0] // chips, -1), "dp", 0, 0, axis_index_groups=chips_of(replicas)
    )
    return jnp.sum(pieces, axis=0)

def gather_rows(x, replicas):
    chips = replicas // CORES
    spread = jnp.broadcast_to(x[None], (chips, *x.shape))
    mine = lax.all_to_all(spread, "dp", 0, 0, axis_index_groups=chips_of(replicas))
    return mine.reshape(chips * x.shape[0], -1)

def sum_over_mp(x):
    ranks = lax.axis_size("mp")
    spread = jnp.broadcast_to(x[None], (ranks, *x.shape))
    return jnp.sum(lax.all_to_all(spread, "mp", 0, 0), axis=0)

SUB = 32
GROUP = 8

def inverse_factor_kernel(gram, out, table):
    rank = gram.shape[0]
    table[:, :rank] = gram[...]
    row = lax.broadcasted_iota(jnp.int32, (rank, rank), 0)
    column = lax.broadcasted_iota(jnp.int32, (rank, rank), 1)
    table[:, rank:] = jnp.where(row == column, 1.0, 0.0)
    shape = (SUB, rank)
    place = lax.broadcasted_iota(jnp.int32, shape, 0)
    for first in range(0, rank, SUB):
        parts = [table[first : first + SUB, :rank], table[first : first + SUB, rank:]]
        for j in range(SUB):
            if j % GROUP == 0:
                columns = [
                    jnp.broadcast_to(parts[0][:, first + k : first + k + 1], shape)
                    for k in range(j, j + GROUP)
                ]
            across = columns.pop(0)
            pivot = across[j : j + 1, :]
            scale = lax.rsqrt(pivot)
            factor = jnp.where(place > j, across * (scale * scale), 0.0)
            columns = [x - factor * x[j : j + 1, :] for x in columns]
            keep = jnp.where(place == j, scale, 1.0)
            parts = [x * keep - factor * x[j : j + 1, :] for x in parts]
        panel = jnp.concatenate(parts, axis=1)
        table[first : first + SUB, :] = panel
        if first + SUB < rank:
            change = lax.dot_general(
                parts[0],
                panel,
                (((0,), (0,)), ((), ())),
                precision=HIGHEST,
                preferred_element_type=F32,
            )
            table[first + SUB :, :] -= change[first + SUB :, :]
    out[...] = table[:, rank:].T

def inverse_factor(gram_matrix):
    rank = gram_matrix.shape[0]
    return pl.pallas_call(
        inverse_factor_kernel,
        out_shape=jax.ShapeDtypeStruct((rank, rank), F32),
        grid=(1,),
        in_specs=[pl.BlockSpec((rank, rank), lambda i: (0, 0))],
        out_specs=pl.BlockSpec((rank, rank), lambda i: (0, 0)),
        scratch_shapes=[pltpu.VMEM((rank, 2 * rank), F32)],
        compiler_params=pltpu.CompilerParams(vmem_limit_bytes=VMEM_LIMIT),
        cost_estimate=pl.CostEstimate(flops=2 * 10**9, bytes_accessed=10**7, transcendentals=128),
        name="inverse_factor",
    )(gram_matrix)

def input_gradient(grad_hidden, up_weight):
    partial_input = dot(grad_hidden, lax.all_gather(up_weight, "dp", axis=0, tiled=True), ((1,), (1,)))
    return lax.psum_scatter(partial_input, "mp", scatter_dimension=1, tiled=True)

def local(activations, grad_hidden, up_weight, error_feedback, query_previous):
    replicas = lax.axis_size("dp")
    error = error_feedback[0]
    replica = lax.axis_index("dp")
    place = jnp.stack([replica % CORES, replica, jnp.int32(replicas)])
    mine, theirs = project_part(place, activations, grad_hidden, error, query_previous)
    own = gather_rows(sum_over_mp(scatter_sum(mine, theirs, replicas)), replicas)
    other = swapped(own, replicas)
    grad_input = input_gradient(grad_hidden, up_weight)
    mine, theirs, gram_matrix = query_part(place, activations, grad_hidden, error, own, other)
    inverse = inverse_factor(gram_matrix)
    query_own = gather_rows(scatter_sum(mine, theirs, replicas), replicas)
    query_own, inverse = lax.optimization_barrier((query_own, inverse))
    query_other = swapped(query_own, replicas)
    error_next, update, query_next = residual(
        place, activations, grad_hidden, error, own, other, inverse, query_own, query_other,
        error.shape[0] // replicas,
    )
    grad_input, error_next = lax.optimization_barrier((grad_input, error_next))
    return (grad_input.astype(BF16), error_next[None], update, query_next)

def solution(mesh):
    in_specs = (P("dp", None), P("dp", "mp"), P("dp", "mp"), P("dp", None, "mp"), P("mp", None))
    out_specs = (P("dp", "mp"), P("dp", None, "mp"), P("dp", "mp"), P("mp", None))
    return jax.shard_map(local, mesh=mesh, in_specs=in_specs, out_specs=out_specs, check_vma=False)
```

```python
import functools

import jax
import jax.numpy as jnp
from jax import lax
from jax.experimental import pallas as pl
from jax.experimental.pallas import tpu as pltpu
from jax.sharding import PartitionSpec as P

HIGHEST = lax.Precision.HIGHEST
F32 = jnp.float32
BF16 = jnp.bfloat16
BLOCK = 640
CORES = 2
VMEM_LIMIT = 48 << 20

def dot(a, b, dims):
    return lax.dot_general(a, b, (dims, ((), ())), preferred_element_type=F32)

def pair(x):
    high = x.astype(BF16)
    rest = (x - high.astype(F32)).astype(BF16)
    return jnp.concatenate([high, rest], axis=1)

def folded(x):
    half = x.shape[1] // 2
    return x[:, :half] + x[:, half:]

def load(source, target, sem):
    copy = pltpu.make_async_copy(source, target, sem)
    copy.start()
    return copy

def row_of(step, core, rows):
    half = rows // CORES
    steps = half // BLOCK
    own = jnp.where(step < steps, core, 1 - core)
    return pl.multiple_of(own * half + lax.rem(step, steps) * BLOCK, BLOCK)

def start_rows(core, error, error_rows, sems):
    rows = error.shape[0]

    def start(step, carry):
        load(error.at[pl.ds(row_of(step, core, rows), BLOCK)], error_rows.at[step], sems.at[step])
        return carry

    lax.fori_loop(0, rows // BLOCK, start, 0)

def wait_rows(step, error, error_rows, sems):
    pltpu.make_async_copy(error.at[pl.ds(0, BLOCK)], error_rows.at[step], sems.at[step]).wait()

def halves(core, rows, body, first, second):
    steps = rows // CORES // BLOCK
    for base, ref in ((0, first), (steps, second)):

        def step_of(i, carry, base=base, ref=ref):
            body(base + i, row_of(base + i, core, rows), pl.multiple_of(i * BLOCK, BLOCK), ref)
            return carry

        lax.fori_loop(0, steps, step_of, 0)

def project_kernel(place, acts, hidden, error, query, mine, theirs,
                   acts_in, hidden_in, query_in, error_rows, query_pair, token_pair, small, sems):
    core = place[0]
    copies = [
        load(query, query_in, small.at[0]),
        load(hidden, hidden_in, small.at[1]),
        load(acts, acts_in, small.at[2]),
    ]
    start_rows(core, error, error_rows, sems)
    copies[0].wait()
    split = pair(query_in[...])
    query_pair[...] = split
    copies[1].wait()
    token_pair[...] = pair(folded(dot(hidden_in[...], split, ((1,), (0,)))))
    copies[2].wait()

    def body(step, row, at, ref):
        wait_rows(step, error, error_rows, sems)
        total = dot(error_rows[step], query_pair[...], ((1,), (0,)))
        total += dot(acts_in[:, pl.ds(row, BLOCK)], token_pair[...], ((0,), (0,)))
        ref[pl.ds(at, BLOCK), :] = folded(total)

    halves(core, error.shape[0], body, mine, theirs)

HBM = pl.BlockSpec(memory_space=pltpu.HBM)
SCALARS = pl.BlockSpec(memory_space=pltpu.SMEM)

def whole(shape):
    return pl.BlockSpec(shape, lambda i: (0,) * len(shape))

def project_part(place, acts, hidden, error, query):
    tokens, rows = acts.shape
    columns, rank = query.shape
    half = (rows // CORES, rank)
    return pl.pallas_call(
        project_kernel,
        grid=(1,),
        in_specs=[SCALARS, HBM, HBM, HBM, HBM],
        out_specs=(whole(half), whole(half)),
        out_shape=(jax.ShapeDtypeStruct(half, F32),) * 2,
        scratch_shapes=[
            pltpu.VMEM((tokens, rows), BF16),
            pltpu.VMEM((tokens, columns), BF16),
            pltpu.VMEM((columns, rank), F32),
            pltpu.VMEM((rows // BLOCK, BLOCK, columns), BF16),
            pltpu.VMEM((columns, 2 * rank), BF16),
            pltpu.VMEM((tokens, 2 * rank), BF16),
            pltpu.SemaphoreType.DMA((3,)),
            pltpu.SemaphoreType.DMA((rows // BLOCK,)),
        ],
        compiler_params=pltpu.CompilerParams(vmem_limit_bytes=60 << 20),
        cost_estimate=pl.CostEstimate(
            flops=4 * rows * columns * rank, bytes_accessed=2 * rows * columns, transcendentals=0
        ),
        name="project_part",
    )(place, acts, hidden, error, query)

def query_kernel(place, acts, hidden, error, own, other, mine, theirs, gram,
                 acts_in, hidden_in, error_rows, total, tokens_sum, gram_sum, small, sems):
    core = place[0]
    rank = gram.shape[0]
    acts_copy = load(acts, acts_in, small.at[0])
    start_rows(core, error, error_rows, sems)
    hidden_copy = load(hidden, hidden_in, small.at[1])
    total[...] = jnp.zeros_like(total)
    tokens_sum[...] = jnp.zeros_like(tokens_sum)
    gram_sum[...] = jnp.zeros_like(gram_sum)
    acts_copy.wait()

    def body(step, row, at, ref):
        split = pair(ref[pl.ds(at, BLOCK), :])
        gram_sum[...] += dot(split, split, ((0,), (0,)))
        tokens_sum[...] += dot(acts_in[:, pl.ds(row, BLOCK)], split, ((1,), (0,)))
        wait_rows(step, error, error_rows, sems)
        total[...] += dot(split, error_rows[step], ((0,), (0,)))

    halves(core, error.shape[0], body, own, other)
    hidden_copy.wait()
    spread = pair(folded(tokens_sum[...]))
    turned = total[...] + dot(spread, hidden_in[...], ((0,), (0,)))
    total[:rank, :] = turned[:rank, :] + turned[rank:, :]
    half = mine.shape[0]
    mine[...] = total[:rank, pl.ds(pl.multiple_of(core * half, half), half)].T
    theirs[...] = total[:rank, pl.ds(pl.multiple_of((1 - core) * half, half), half)].T
    gram[...] = folded(gram_sum[:rank, :] + gram_sum[rank:, :])

def query_part(place, acts, hidden, error, own, other):
    tokens, rows = acts.shape
    columns = hidden.shape[1]
    rank = own.shape[1]
    half = (columns // CORES, rank)
    return pl.pallas_call(
        query_kernel,
        grid=(1,),
        in_specs=[SCALARS, HBM, HBM, HBM, whole(own.shape), whole(own.shape)],
        out_specs=(whole(half), whole(half), whole((rank, rank))),
        out_shape=(
            jax.ShapeDtypeStruct(half, F32),
            jax.ShapeDtypeStruct(half, F32),
            jax.ShapeDtypeStruct((rank, rank), F32),
        ),
        scratch_shapes=[
            pltpu.VMEM((tokens, rows), BF16),
            pltpu.VMEM((tokens, columns), BF16),
            pltpu.VMEM((rows // BLOCK, BLOCK, columns), BF16),
            pltpu.VMEM((2 * rank, columns), F32),
            pltpu.VMEM((tokens, 2 * rank), F32),
            pltpu.VMEM((2 * rank, 2 * rank), F32),
            pltpu.SemaphoreType.DMA((2,)),
            pltpu.SemaphoreType.DMA((rows // BLOCK,)),
        ],
        compiler_params=pltpu.CompilerParams(vmem_limit_bytes=VMEM_LIMIT),
        cost_estimate=pl.CostEstimate(
            flops=4 * rows * columns * rank, bytes_accessed=2 * rows * columns, transcendentals=0
        ),
        name="query_part",
    )(place, acts, hidden, error, own, other)

def triple(x):
    split = pair(x)
    return jnp.concatenate([split, split[:, : x.shape[1]]], axis=1)

def stacked(x):
    high = x.astype(BF16)
    rest = (x - high.astype(F32)).astype(BF16)
    return jnp.concatenate([high, high, rest], axis=0)

def residual_kernel(place, acts, hidden, error, own, other, inverse, query_own, query_other,
                    out, update, query,
                    acts_in, hidden_in, error_rows, turn, factors, small, sems, sent):
    core, replica, replicas = place[0], place[1], place[2]
    rank = inverse.shape[0]
    rows = error.shape[0]
    acts_copy = load(acts, acts_in, small.at[0])
    hidden_copy = load(hidden, hidden_in, small.at[1])
    start_rows(core, error, error_rows, sems)
    turn[...] = stacked(inverse[...])
    scale = 1.0 / replicas.astype(F32)
    half = query_own.shape[0]
    for ref, first in ((query_own, core * half), (query_other, (1 - core) * half)):
        query[pl.ds(pl.multiple_of(first, half), half), :] = (
            dot(triple(ref[...]), turn[...], ((1,), (0,))) * scale
        )
    factors[: 3 * rank, :] = stacked(query[...].T)
    hidden_copy.wait()
    factors[3 * rank :, :] = -hidden_in[...]
    share = update.shape[0]
    first = replica * share
    within = lax.rem(first, rows // CORES)
    at = pl.ds(pl.multiple_of(within, 8), share)
    own_half = jnp.where(first < rows // CORES, 0, 1) == core
    picked = jnp.where(own_half, own[at, :], other[at, :])
    basis = dot(triple(picked), turn[...], ((1,), (0,)))
    update[...] = dot(triple(basis), factors[: 3 * rank, :], ((1,), (0,)))
    acts_copy.wait()

    def body(step, row, at, ref):
        basis = dot(triple(ref[pl.ds(at, BLOCK), :]), turn[...], ((1,), (0,)))
        mixed = jnp.concatenate([triple(basis), acts_in[:, pl.ds(row, BLOCK)].T], axis=1)
        change = dot(mixed, factors[...], ((1,), (0,)))
        wait_rows(step, error, error_rows, sems)
        error_rows[step] = (error_rows[step].astype(F32) - change).astype(BF16)
        load(error_rows.at[step], out.at[pl.ds(row, BLOCK)], sent.at[step])

    halves(core, rows, body, own, other)

    def drain(step, carry):
        pltpu.make_async_copy(error_rows.at[step], out.at[pl.ds(0, BLOCK)], sent.at[step]).wait()
        return carry

    lax.fori_loop(0, rows // BLOCK, drain, 0)

def residual(place, acts, hidden, error, own, other, inverse, query_own, query_other, share):
    tokens, rows = acts.shape
    columns = hidden.shape[1]
    rank = inverse.shape[0]
    return pl.pallas_call(
        residual_kernel,
        grid=(1,),
        in_specs=[
            SCALARS, HBM, HBM, HBM, whole(own.shape), whole(own.shape), whole(inverse.shape),
            whole(query_own.shape), whole(query_own.shape),
        ],
        out_specs=(HBM, whole((share, columns)), whole((columns, rank))),
        out_shape=(
            jax.ShapeDtypeStruct((rows, columns), BF16),
            jax.ShapeDtypeStruct((share, columns), F32),
            jax.ShapeDtypeStruct((columns, rank), F32),
        ),
        scratch_shapes=[
            pltpu.VMEM((tokens, rows), BF16),
            pltpu.VMEM((tokens, columns), BF16),
            pltpu.VMEM((rows // BLOCK, BLOCK, columns), BF16),
            pltpu.VMEM((3 * rank, rank), BF16),
            pltpu.VMEM((3 * rank + tokens, columns), BF16),
            pltpu.SemaphoreType.DMA((2,)),
            pltpu.SemaphoreType.DMA((rows // BLOCK,)),
            pltpu.SemaphoreType.DMA((rows // BLOCK,)),
        ],
        compiler_params=pltpu.CompilerParams(vmem_limit_bytes=VMEM_LIMIT),
        cost_estimate=pl.CostEstimate(
            flops=8 * rows * columns * rank, bytes_accessed=4 * rows * columns, transcendentals=0
        ),
        name="residual",
    )(place, acts, hidden, error, own, other, inverse, query_own, query_other)


def chips_of(replicas):
    return [list(range(core, replicas, CORES)) for core in range(CORES)]

def swapped(x, replicas):
    return lax.ppermute(x, "dp", [(i, i ^ 1) for i in range(replicas)])

def scatter_sum(x, replicas):
    chips = replicas // CORES
    pieces = lax.all_to_all(
        x.reshape(chips, x.shape[0] // chips, -1), "dp", 0, 0, axis_index_groups=chips_of(replicas)
    )
    return jnp.sum(pieces, axis=0)


def gather_rows(x, replicas):
    chips = replicas // CORES
    spread = jnp.broadcast_to(x[None], (chips, *x.shape))
    mine = lax.all_to_all(spread, "dp", 0, 0, axis_index_groups=chips_of(replicas))
    return mine.reshape(chips * x.shape[0], -1)

def sum_over_mp(x):
    ranks = lax.axis_size("mp")
    spread = jnp.broadcast_to(x[None], (ranks, *x.shape))
    return jnp.sum(lax.all_to_all(spread, "mp", 0, 0), axis=0)

SUB = 32
GROUP = 8

def inverse_factor_kernel(gram, out, table):
    rank = gram.shape[0]
    table[:, :rank] = gram[...]
    row = lax.broadcasted_iota(jnp.int32, (rank, rank), 0)
    column = lax.broadcasted_iota(jnp.int32, (rank, rank), 1)
    table[:, rank:] = jnp.where(row == column, 1.0, 0.0)
    shape = (SUB, rank)
    place = lax.broadcasted_iota(jnp.int32, shape, 0)
    for first in range(0, rank, SUB):
        parts = [table[first : first + SUB, :rank], table[first : first + SUB, rank:]]
        for j in range(SUB):
            if j % GROUP == 0:
                columns = [
                    jnp.broadcast_to(parts[0][:, first + k : first + k + 1], shape)
                    for k in range(j, j + GROUP)
                ]
            across = columns.pop(0)
            pivot = across[j : j + 1, :]
            scale = lax.rsqrt(pivot)
            factor = jnp.where(place > j, across * (scale * scale), 0.0)
            columns = [x - factor * x[j : j + 1, :] for x in columns]
            keep = jnp.where(place == j, scale, 1.0)
            parts = [x * keep - factor * x[j : j + 1, :] for x in parts]
        panel = jnp.concatenate(parts, axis=1)
        table[first : first + SUB, :] = panel
        if first + SUB < rank:
            change = lax.dot_general(
                parts[0],
                panel,
                (((0,), (0,)), ((), ())),
                precision=HIGHEST,
                preferred_element_type=F32,
            )
            table[first + SUB :, :] -= change[first + SUB :, :]
    out[...] = table[:, rank:].T

def inverse_factor(gram_matrix):
    rank = gram_matrix.shape[0]
    return pl.pallas_call(
        inverse_factor_kernel,
        out_shape=jax.ShapeDtypeStruct((rank, rank), F32),
        grid=(1,),
        in_specs=[pl.BlockSpec((rank, rank), lambda i: (0, 0))],
        out_specs=pl.BlockSpec((rank, rank), lambda i: (0, 0)),
        scratch_shapes=[pltpu.VMEM((rank, 2 * rank), F32)],
        compiler_params=pltpu.CompilerParams(vmem_limit_bytes=VMEM_LIMIT),
        cost_estimate=pl.CostEstimate(flops=2 * 10**9, bytes_accessed=10**7, transcendentals=128),
        name="inverse_factor",
    )(gram_matrix)

def gradient_kernel(place, *refs):
    core, across, down = place[0], place[3], place[4]
    tokens, weights, out, table = refs[:WIDE], refs[WIDE : WIDE + HIGH], refs[-2], refs[-1]
    share = weights[0].shape[0] // CORES
    count = tokens[0].shape[0]
    for d, ref in enumerate(tokens):
        table[d * count : (d + 1) * count, :] = ref[...]
    for e, ref in enumerate(weights):
        block = dot(ref[...], table[...], ((1,), (1,)))
        y = lax.rem(down - e + HIGH, HIGH)
        for d in range(WIDE):
            x = lax.rem(across - d + WIDE, WIDE)
            for side, of_core in ((0, core), (1, 1 - core)):
                at = pl.ds(pl.multiple_of(of_core * share, 8), share)
                out[y, x, at, :] = block[
                    side * share : (side + 1) * share, d * count : (d + 1) * count
                ]


def gradient_part(place, tokens, weights):
    count, columns = tokens[0].shape
    rows = weights[0].shape[0]
    return pl.pallas_call(
        gradient_kernel,
        grid=(1,),
        in_specs=[SCALARS, *(whole(x.shape) for x in (*tokens, *weights))],
        out_specs=whole((HIGH, WIDE, rows, count)),
        out_shape=jax.ShapeDtypeStruct((HIGH, WIDE, rows, count), F32),
        scratch_shapes=[pltpu.VMEM((WIDE * count, columns), BF16)],
        compiler_params=pltpu.CompilerParams(vmem_limit_bytes=60 << 20),
        cost_estimate=pl.CostEstimate(
            flops=2 * WIDE * HIGH * rows * count * columns, bytes_accessed=10**7, transcendentals=0
        ),
        name="gradient_part",
    )(place, *tokens, *weights)


WIDE = 4
HIGH = 4


def index_of(y, x, core):
    return (y % HIGH * WIDE + x % WIDE) * CORES + core


def shifted(x, replicas, rows, columns):
    pairs = []
    for i in range(replicas):
        at, core = divmod(i, CORES)
        y, across = divmod(at, WIDE)
        pairs.append((i, index_of(y + rows, across + columns, core)))
    return lax.ppermute(x, "dp", pairs)


def after(x, earlier):
    return lax.optimization_barrier((x, earlier))[0]


def split_step(x, bit, distance, axis):
    ranks = lax.axis_size("mp")
    keep = lax.dynamic_index_in_dim(x, bit, axis, keepdims=False)
    send = lax.dynamic_index_in_dim(x, 1 - bit, axis, keepdims=False)
    return keep, lax.ppermute(send, "mp", [(i, i ^ distance) for i in range(ranks)])


def settle(x, replicas):
    ranks = lax.axis_size("mp")
    across = lax.axis_index("dp") // CORES % WIDE
    low = across % 2
    got = []
    for flip in range(2):
        pairs = []
        for i in range(replicas):
            at, core = divmod(i, CORES)
            y, column = divmod(at, WIDE)
            for z in range(ranks):
                to = index_of(y, 2 * (z % 2) + (column % 2 ^ flip), core)
                pairs.append((i * ranks + z, to * ranks + (z // 2 * 2 + column // 2)))
        piece = lax.dynamic_index_in_dim(x, low ^ flip, 0, keepdims=False)
        got.append(lax.ppermute(piece, ("dp", "mp"), pairs))
    return got, low


def local(activations, grad_hidden, up_weight, error_feedback, query_previous):
    replicas = lax.axis_size("dp")
    error = error_feedback[0]
    replica = lax.axis_index("dp")
    plane = lax.axis_index("mp")
    chip = replica // CORES
    place = jnp.stack(
        [replica % CORES, replica, jnp.int32(replicas), chip % WIDE, chip // WIDE]
    )
    rows = jnp.concatenate([up_weight, swapped(up_weight, replicas)], axis=0)
    mine, theirs = project_part(place, activations, grad_hidden, error, query_previous)
    mine = mine + swapped(theirs, replicas)

    rows, hidden, mine = lax.optimization_barrier((rows, grad_hidden, mine))
    tokens = [hidden] + [shifted(hidden, replicas, 0, d) for d in range(1, WIDE)]
    weights = [rows] + [shifted(rows, replicas, e, 0) for e in range(1, HIGH)]
    share = sum_over_mp(scatter_sum(mine, replicas))
    tokens, weights, share = lax.optimization_barrier((tokens, weights, share))

    own = gather_rows(share, replicas)
    part = gradient_part(place, tokens, weights)
    own, part = lax.optimization_barrier((own, part))
    part = part.reshape(HIGH, 2, -1, part.shape[-1])
    keep, sent = split_step(part, plane % 2, 1, 1)
    other = swapped(own, replicas)
    mine, theirs, gram_matrix = query_part(place, activations, grad_hidden, error, own, other)
    inverse = inverse_factor(gram_matrix)

    part = (after(keep, gram_matrix) + sent).reshape(HIGH // 2, 2, *keep.shape[1:])
    keep, sent = split_step(part, plane // 2 % 2, 2, 1)
    query_share = scatter_sum(mine + swapped(theirs, replicas), replicas)
    part = after(keep, query_share) + sent
    keep, sent = split_step(part, plane // 4, 4, 0)
    query_own = gather_rows(query_share, replicas)
    query_own, inverse = lax.optimization_barrier((query_own, inverse))
    part = (after(keep, query_own) + sent).astype(BF16)
    got, low = settle(part.reshape(2, -1, part.shape[-1]), replicas)
    query_other = swapped(query_own, replicas)
    error_next, update, query_next = residual(
        place, activations, grad_hidden, error, own, other, inverse, query_own, query_other,
        error.shape[0] // replicas,
    )
    got = after(got, error_next)
    grad_input = jnp.where(
        low == 0, jnp.concatenate(got, axis=0), jnp.concatenate(got[::-1], axis=0)
    ).T
    return (grad_input, error_next[None], update, query_next)


def solution(mesh):
    in_specs = (P("dp", None), P("dp", "mp"), P("dp", "mp"), P("dp", None, "mp"), P("mp", None))
    out_specs = (P("dp", "mp"), P("dp", None, "mp"), P("dp", "mp"), P("mp", None))
    return jax.shard_map(local, mesh=mesh, in_specs=in_specs, out_specs=out_specs, check_vma=False)
```

```python
import functools

import jax
import jax.numpy as jnp
from jax import lax
from jax.experimental import pallas as pl
from jax.experimental.pallas import tpu as pltpu
from jax.sharding import PartitionSpec as P

HIGHEST = lax.Precision.HIGHEST
F32 = jnp.float32
BF16 = jnp.bfloat16
BLOCK = 640
CORES = 2
VMEM_LIMIT = 48 << 20

def dot(a, b, dims):
    return lax.dot_general(a, b, (dims, ((), ())), preferred_element_type=F32)

def pair(x):
    high = x.astype(BF16)
    rest = (x - high.astype(F32)).astype(BF16)
    return jnp.concatenate([high, rest], axis=1)

def folded(x):
    half = x.shape[1] // 2
    return x[:, :half] + x[:, half:]

def load(source, target, sem):
    copy = pltpu.make_async_copy(source, target, sem)
    copy.start()
    return copy

def row_of(step, core, rows):
    half = rows // CORES
    steps = half // BLOCK
    own = jnp.where(step < steps, core, 1 - core)
    return pl.multiple_of(own * half + lax.rem(step, steps) * BLOCK, BLOCK)

def start_rows(core, error, error_rows, sems):
    rows = error.shape[0]

    def start(step, carry):
        load(error.at[pl.ds(row_of(step, core, rows), BLOCK)], error_rows.at[step], sems.at[step])
        return carry

    lax.fori_loop(0, rows // BLOCK, start, 0)

def wait_rows(step, error, error_rows, sems):
    pltpu.make_async_copy(error.at[pl.ds(0, BLOCK)], error_rows.at[step], sems.at[step]).wait()

def halves(core, rows, body, first, second):
    steps = rows // CORES // BLOCK
    for base, ref in ((0, first), (steps, second)):

        def step_of(i, carry, base=base, ref=ref):
            body(base + i, row_of(base + i, core, rows), pl.multiple_of(i * BLOCK, BLOCK), ref)
            return carry

        lax.fori_loop(0, steps, step_of, 0)

def project_kernel(place, acts, hidden, error, query, mine, theirs,
                   acts_in, hidden_in, query_in, error_rows, query_pair, token_pair, small, sems):
    core = place[0]
    copies = [
        load(query, query_in, small.at[0]),
        load(hidden, hidden_in, small.at[1]),
        load(acts, acts_in, small.at[2]),
    ]
    start_rows(core, error, error_rows, sems)
    copies[0].wait()
    split = pair(query_in[...])
    query_pair[...] = split
    copies[1].wait()
    token_pair[...] = pair(folded(dot(hidden_in[...], split, ((1,), (0,)))))
    copies[2].wait()

    def body(step, row, at, ref):
        wait_rows(step, error, error_rows, sems)
        total = dot(error_rows[step], query_pair[...], ((1,), (0,)))
        total += dot(acts_in[:, pl.ds(row, BLOCK)], token_pair[...], ((0,), (0,)))
        ref[pl.ds(at, BLOCK), :] = folded(total)

    halves(core, error.shape[0], body, mine, theirs)

HBM = pl.BlockSpec(memory_space=pltpu.HBM)
SCALARS = pl.BlockSpec(memory_space=pltpu.SMEM)

def whole(shape):
    return pl.BlockSpec(shape, lambda i: (0,) * len(shape))

def project_part(place, acts, hidden, error, query):
    tokens, rows = acts.shape
    columns, rank = query.shape
    half = (rows // CORES, rank)
    return pl.pallas_call(
        project_kernel,
        grid=(1,),
        in_specs=[SCALARS, HBM, HBM, HBM, HBM],
        out_specs=(whole(half), whole(half)),
        out_shape=(jax.ShapeDtypeStruct(half, F32),) * 2,
        scratch_shapes=[
            pltpu.VMEM((tokens, rows), BF16),
            pltpu.VMEM((tokens, columns), BF16),
            pltpu.VMEM((columns, rank), F32),
            pltpu.VMEM((rows // BLOCK, BLOCK, columns), BF16),
            pltpu.VMEM((columns, 2 * rank), BF16),
            pltpu.VMEM((tokens, 2 * rank), BF16),
            pltpu.SemaphoreType.DMA((3,)),
            pltpu.SemaphoreType.DMA((rows // BLOCK,)),
        ],
        compiler_params=pltpu.CompilerParams(vmem_limit_bytes=60 << 20),
        cost_estimate=pl.CostEstimate(
            flops=4 * rows * columns * rank, bytes_accessed=2 * rows * columns, transcendentals=0
        ),
        name="project_part",
    )(place, acts, hidden, error, query)

def query_kernel(place, acts, hidden, error, own, other, mine, theirs, gram,
                 acts_in, hidden_in, error_rows, total, tokens_sum, gram_sum, small, sems):
    core = place[0]
    rank = gram.shape[0]
    acts_copy = load(acts, acts_in, small.at[0])
    start_rows(core, error, error_rows, sems)
    hidden_copy = load(hidden, hidden_in, small.at[1])
    total[...] = jnp.zeros_like(total)
    tokens_sum[...] = jnp.zeros_like(tokens_sum)
    gram_sum[...] = jnp.zeros_like(gram_sum)
    acts_copy.wait()

    def body(step, row, at, ref):
        split = pair(ref[pl.ds(at, BLOCK), :])
        gram_sum[...] += dot(split, split, ((0,), (0,)))
        tokens_sum[...] += dot(acts_in[:, pl.ds(row, BLOCK)], split, ((1,), (0,)))
        wait_rows(step, error, error_rows, sems)
        total[...] += dot(split, error_rows[step], ((0,), (0,)))

    halves(core, error.shape[0], body, own, other)
    hidden_copy.wait()
    spread = pair(folded(tokens_sum[...]))
    turned = total[...] + dot(spread, hidden_in[...], ((0,), (0,)))
    total[:rank, :] = turned[:rank, :] + turned[rank:, :]
    half = mine.shape[0]
    mine[...] = total[:rank, pl.ds(pl.multiple_of(core * half, half), half)].T
    theirs[...] = total[:rank, pl.ds(pl.multiple_of((1 - core) * half, half), half)].T
    gram[...] = folded(gram_sum[:rank, :] + gram_sum[rank:, :])

def query_part(place, acts, hidden, error, own, other):
    tokens, rows = acts.shape
    columns = hidden.shape[1]
    rank = own.shape[1]
    half = (columns // CORES, rank)
    return pl.pallas_call(
        query_kernel,
        grid=(1,),
        in_specs=[SCALARS, HBM, HBM, HBM, whole(own.shape), whole(own.shape)],
        out_specs=(whole(half), whole(half), whole((rank, rank))),
        out_shape=(
            jax.ShapeDtypeStruct(half, F32),
            jax.ShapeDtypeStruct(half, F32),
            jax.ShapeDtypeStruct((rank, rank), F32),
        ),
        scratch_shapes=[
            pltpu.VMEM((tokens, rows), BF16),
            pltpu.VMEM((tokens, columns), BF16),
            pltpu.VMEM((rows // BLOCK, BLOCK, columns), BF16),
            pltpu.VMEM((2 * rank, columns), F32),
            pltpu.VMEM((tokens, 2 * rank), F32),
            pltpu.VMEM((2 * rank, 2 * rank), F32),
            pltpu.SemaphoreType.DMA((2,)),
            pltpu.SemaphoreType.DMA((rows // BLOCK,)),
        ],
        compiler_params=pltpu.CompilerParams(vmem_limit_bytes=VMEM_LIMIT),
        cost_estimate=pl.CostEstimate(
            flops=4 * rows * columns * rank, bytes_accessed=2 * rows * columns, transcendentals=0
        ),
        name="query_part",
    )(place, acts, hidden, error, own, other)

def triple(x):
    split = pair(x)
    return jnp.concatenate([split, split[:, : x.shape[1]]], axis=1)

def stacked(x):
    high = x.astype(BF16)
    rest = (x - high.astype(F32)).astype(BF16)
    return jnp.concatenate([high, high, rest], axis=0)

def residual_kernel(place, acts, hidden, error, own, other, inverse, query_own, query_other,
                    out, update, query,
                    acts_in, hidden_in, error_rows, turn, factors, small, sems, sent):
    core, replica, replicas = place[0], place[1], place[2]
    rank = inverse.shape[0]
    rows = error.shape[0]
    acts_copy = load(acts, acts_in, small.at[0])
    hidden_copy = load(hidden, hidden_in, small.at[1])
    start_rows(core, error, error_rows, sems)
    turn[...] = stacked(inverse[...])
    scale = 1.0 / replicas.astype(F32)
    half = query_own.shape[0]
    for ref, first in ((query_own, core * half), (query_other, (1 - core) * half)):
        query[pl.ds(pl.multiple_of(first, half), half), :] = (
            dot(triple(ref[...]), turn[...], ((1,), (0,))) * scale
        )
    factors[: 3 * rank, :] = stacked(query[...].T)
    hidden_copy.wait()
    factors[3 * rank :, :] = -hidden_in[...]
    share = update.shape[0]
    first = replica * share
    within = lax.rem(first, rows // CORES)
    at = pl.ds(pl.multiple_of(within, 8), share)
    own_half = jnp.where(first < rows // CORES, 0, 1) == core
    picked = jnp.where(own_half, own[at, :], other[at, :])
    basis = dot(triple(picked), turn[...], ((1,), (0,)))
    update[...] = dot(triple(basis), factors[: 3 * rank, :], ((1,), (0,)))
    acts_copy.wait()

    def body(step, row, at, ref):
        basis = dot(triple(ref[pl.ds(at, BLOCK), :]), turn[...], ((1,), (0,)))
        mixed = jnp.concatenate([triple(basis), acts_in[:, pl.ds(row, BLOCK)].T], axis=1)
        change = dot(mixed, factors[...], ((1,), (0,)))
        wait_rows(step, error, error_rows, sems)
        error_rows[step] = (error_rows[step].astype(F32) - change).astype(BF16)
        load(error_rows.at[step], out.at[pl.ds(row, BLOCK)], sent.at[step])

    halves(core, rows, body, own, other)

    def drain(step, carry):
        pltpu.make_async_copy(error_rows.at[step], out.at[pl.ds(0, BLOCK)], sent.at[step]).wait()
        return carry

    lax.fori_loop(0, rows // BLOCK, drain, 0)

def residual(place, acts, hidden, error, own, other, inverse, query_own, query_other, share):
    tokens, rows = acts.shape
    columns = hidden.shape[1]
    rank = inverse.shape[0]
    return pl.pallas_call(
        residual_kernel,
        grid=(1,),
        in_specs=[
            SCALARS, HBM, HBM, HBM, whole(own.shape), whole(own.shape), whole(inverse.shape),
            whole(query_own.shape), whole(query_own.shape),
        ],
        out_specs=(HBM, whole((share, columns)), whole((columns, rank))),
        out_shape=(
            jax.ShapeDtypeStruct((rows, columns), BF16),
            jax.ShapeDtypeStruct((share, columns), F32),
            jax.ShapeDtypeStruct((columns, rank), F32),
        ),
        scratch_shapes=[
            pltpu.VMEM((tokens, rows), BF16),
            pltpu.VMEM((tokens, columns), BF16),
            pltpu.VMEM((rows // BLOCK, BLOCK, columns), BF16),
            pltpu.VMEM((3 * rank, rank), BF16),
            pltpu.VMEM((3 * rank + tokens, columns), BF16),
            pltpu.SemaphoreType.DMA((2,)),
            pltpu.SemaphoreType.DMA((rows // BLOCK,)),
            pltpu.SemaphoreType.DMA((rows // BLOCK,)),
        ],
        compiler_params=pltpu.CompilerParams(vmem_limit_bytes=VMEM_LIMIT),
        cost_estimate=pl.CostEstimate(
            flops=8 * rows * columns * rank, bytes_accessed=4 * rows * columns, transcendentals=0
        ),
        name="residual",
    )(place, acts, hidden, error, own, other, inverse, query_own, query_other)


def chips_of(replicas):
    return [list(range(core, replicas, CORES)) for core in range(CORES)]

def swapped(x, replicas):
    return lax.ppermute(x, "dp", [(i, i ^ 1) for i in range(replicas)])

def scatter_sum(x, replicas):
    chips = replicas // CORES
    pieces = lax.all_to_all(
        x.reshape(chips, x.shape[0] // chips, -1), "dp", 0, 0, axis_index_groups=chips_of(replicas)
    )
    return jnp.sum(pieces, axis=0)


def gather_rows(x, replicas):
    chips = replicas // CORES
    spread = jnp.broadcast_to(x[None], (chips, *x.shape))
    mine = lax.all_to_all(spread, "dp", 0, 0, axis_index_groups=chips_of(replicas))
    return mine.reshape(chips * x.shape[0], -1)

def sum_over_mp(x):
    ranks = lax.axis_size("mp")
    spread = jnp.broadcast_to(x[None], (ranks, *x.shape))
    return jnp.sum(lax.all_to_all(spread, "mp", 0, 0), axis=0)

SUB = 32
GROUP = 8

def inverse_factor_kernel(gram, out, table):
    rank = gram.shape[0]
    table[:, :rank] = gram[...]
    row = lax.broadcasted_iota(jnp.int32, (rank, rank), 0)
    column = lax.broadcasted_iota(jnp.int32, (rank, rank), 1)
    table[:, rank:] = jnp.where(row == column, 1.0, 0.0)
    shape = (SUB, rank)
    place = lax.broadcasted_iota(jnp.int32, shape, 0)
    for first in range(0, rank, SUB):
        parts = [table[first : first + SUB, :rank], table[first : first + SUB, rank:]]
        for j in range(SUB):
            if j % GROUP == 0:
                columns = [
                    jnp.broadcast_to(parts[0][:, first + k : first + k + 1], shape)
                    for k in range(j, j + GROUP)
                ]
            across = columns.pop(0)
            pivot = across[j : j + 1, :]
            scale = lax.rsqrt(pivot)
            factor = jnp.where(place > j, across * (scale * scale), 0.0)
            columns = [x - factor * x[j : j + 1, :] for x in columns]
            keep = jnp.where(place == j, scale, 1.0)
            parts = [x * keep - factor * x[j : j + 1, :] for x in parts]
        panel = jnp.concatenate(parts, axis=1)
        table[first : first + SUB, :] = panel
        if first + SUB < rank:
            change = lax.dot_general(
                parts[0],
                panel,
                (((0,), (0,)), ((), ())),
                precision=HIGHEST,
                preferred_element_type=F32,
            )
            table[first + SUB :, :] -= change[first + SUB :, :]
    out[...] = table[:, rank:].T

def inverse_factor(gram_matrix):
    rank = gram_matrix.shape[0]
    return pl.pallas_call(
        inverse_factor_kernel,
        out_shape=jax.ShapeDtypeStruct((rank, rank), F32),
        grid=(1,),
        in_specs=[pl.BlockSpec((rank, rank), lambda i: (0, 0))],
        out_specs=pl.BlockSpec((rank, rank), lambda i: (0, 0)),
        scratch_shapes=[pltpu.VMEM((rank, 2 * rank), F32)],
        compiler_params=pltpu.CompilerParams(vmem_limit_bytes=VMEM_LIMIT),
        cost_estimate=pl.CostEstimate(flops=2 * 10**9, bytes_accessed=10**7, transcendentals=128),
        name="inverse_factor",
    )(gram_matrix)

def after(x, earlier):
    return lax.optimization_barrier((x, earlier))[0]


def local(activations, grad_hidden, up_weight, error_feedback, query_previous):
    replicas = lax.axis_size("dp")
    error = error_feedback[0]
    replica = lax.axis_index("dp")
    place = jnp.stack([replica % CORES, replica, jnp.int32(replicas)])
    mine, theirs = project_part(place, activations, grad_hidden, error, query_previous)
    mine = mine + swapped(theirs, replicas)
    own = gather_rows(sum_over_mp(scatter_sum(mine, replicas)), replicas)
    other = swapped(own, replicas)
    mine, theirs, gram_matrix = query_part(place, activations, grad_hidden, error, own, other)
    inverse = inverse_factor(gram_matrix)
    weight = lax.all_gather(up_weight, "dp", axis=0, tiled=True)
    partial_input = dot(after(grad_hidden, gram_matrix), weight, ((1,), (1,)))
    mine = after(mine + swapped(theirs, replicas), partial_input[0, 0])
    grad_input = lax.psum_scatter(partial_input, "mp", scatter_dimension=1, tiled=True)
    query_own = gather_rows(scatter_sum(mine, replicas), replicas)
    query_own, inverse = lax.optimization_barrier((query_own, inverse))
    query_other = swapped(query_own, replicas)
    error_next, update, query_next = residual(
        place, activations, grad_hidden, error, own, other, inverse, query_own, query_other,
        error.shape[0] // replicas,
    )
    grad_input, error_next = lax.optimization_barrier((grad_input, error_next))
    return (grad_input.astype(BF16), error_next[None], update, query_next)

def solution(mesh):
    in_specs = (P("dp", None), P("dp", "mp"), P("dp", "mp"), P("dp", None, "mp"), P("mp", None))
    out_specs = (P("dp", "mp"), P("dp", None, "mp"), P("dp", "mp"), P("mp", None))
    return jax.shard_map(local, mesh=mesh, in_specs=in_specs, out_specs=out_specs, check_vma=False)
```

```python
import functools

import jax
import jax.numpy as jnp
from jax import lax
from jax.experimental import pallas as pl
from jax.experimental.pallas import tpu as pltpu
from jax.sharding import PartitionSpec as P

HIGHEST = lax.Precision.HIGHEST
F32 = jnp.float32
BF16 = jnp.bfloat16
BLOCK = 640
HALF = 1280
CORES = 2
VMEM_LIMIT = 48 << 20

def dot(a, b, dims):
    return lax.dot_general(a, b, (dims, ((), ())), preferred_element_type=F32)

def pair(x):
    high = x.astype(BF16)
    rest = (x - high.astype(F32)).astype(BF16)
    return jnp.concatenate([high, rest], axis=1)

def folded(x):
    half = x.shape[1] // 2
    return x[:, :half] + x[:, half:]

def load(source, target, sem):
    copy = pltpu.make_async_copy(source, target, sem)
    copy.start()
    return copy

def row_of(step, core, rows, block):
    half = rows // CORES
    steps = half // block
    own = jnp.where(step < steps, core, 1 - core)
    return pl.multiple_of(own * half + lax.rem(step, steps) * block, block)

def start_rows(core, error, error_rows, sems):
    rows, (steps, block, _) = error.shape[0], error_rows.shape

    def start(step, carry):
        load(error.at[pl.ds(row_of(step, core, rows, block), block)], error_rows.at[step], sems.at[step])
        return carry

    lax.fori_loop(0, steps, start, 0)

def wait_rows(step, error, error_rows, sems):
    pltpu.make_async_copy(error.at[pl.ds(0, error_rows.shape[1])], error_rows.at[step], sems.at[step]).wait()

def halves(core, rows, block, body, first, second):
    steps = rows // CORES // block
    for base, ref in ((0, first), (steps, second)):

        def step_of(i, carry, base=base, ref=ref):
            body(base + i, row_of(base + i, core, rows, block), pl.multiple_of(i * block, block), ref)
            return carry

        lax.fori_loop(0, steps, step_of, 0)

def project_kernel(acts, hidden, error, query, mine, theirs,
                   acts_in, hidden_in, query_in, error_rows, query_pair, token_pair, small, sems):
    core = lax.rem(lax.axis_index("dp"), CORES)
    copies = [
        load(query, query_in, small.at[0]),
        load(hidden, hidden_in, small.at[1]),
        load(acts, acts_in, small.at[2]),
    ]
    start_rows(core, error, error_rows, sems)
    copies[0].wait()
    split = pair(query_in[...])
    query_pair[...] = split
    copies[1].wait()
    token_pair[...] = pair(folded(dot(hidden_in[...], split, ((1,), (0,)))))
    copies[2].wait()

    def body(step, row, at, ref):
        wait_rows(step, error, error_rows, sems)
        total = dot(error_rows[step], query_pair[...], ((1,), (0,)))
        total += dot(acts_in[:, pl.ds(row, BLOCK)], token_pair[...], ((0,), (0,)))
        ref[pl.ds(at, BLOCK), :] = folded(total)

    halves(core, error.shape[0], BLOCK, body, mine, theirs)

HBM = pl.BlockSpec(memory_space=pltpu.HBM)

def whole(shape):
    return pl.BlockSpec(shape, lambda i: (0,) * len(shape))

def project_part(acts, hidden, error, query):
    tokens, rows = acts.shape
    columns, rank = query.shape
    half = (rows // CORES, rank)
    return pl.pallas_call(
        project_kernel,
        grid=(1,),
        in_specs=[HBM, HBM, HBM, HBM],
        out_specs=(whole(half), whole(half)),
        out_shape=(jax.ShapeDtypeStruct(half, F32),) * 2,
        scratch_shapes=[
            pltpu.VMEM((tokens, rows), BF16),
            pltpu.VMEM((tokens, columns), BF16),
            pltpu.VMEM((columns, rank), F32),
            pltpu.VMEM((rows // BLOCK, BLOCK, columns), BF16),
            pltpu.VMEM((columns, 2 * rank), BF16),
            pltpu.VMEM((tokens, 2 * rank), BF16),
            pltpu.SemaphoreType.DMA((3,)),
            pltpu.SemaphoreType.DMA((rows // BLOCK,)),
        ],
        compiler_params=pltpu.CompilerParams(vmem_limit_bytes=60 << 20),
        cost_estimate=pl.CostEstimate(
            flops=4 * rows * columns * rank, bytes_accessed=2 * rows * columns, transcendentals=0
        ),
        name="project_part",
    )(acts, hidden, error, query)

def query_kernel(acts, hidden, error, own, other, mine, theirs, gram,
                 acts_in, hidden_in, error_rows, total, tokens_sum, gram_sum, small, sems):
    core = lax.rem(lax.axis_index("dp"), CORES)
    rank = gram.shape[0]
    acts_copy = load(acts, acts_in, small.at[0])
    start_rows(core, error, error_rows, sems)
    hidden_copy = load(hidden, hidden_in, small.at[1])
    total[...] = jnp.zeros_like(total)
    tokens_sum[...] = jnp.zeros_like(tokens_sum)
    gram_sum[...] = jnp.zeros_like(gram_sum)
    acts_copy.wait()

    def body(step, row, at, ref):
        split = pair(ref[pl.ds(at, HALF), :])
        gram_sum[...] += dot(split, split, ((0,), (0,)))
        tokens_sum[...] += dot(acts_in[:, pl.ds(row, HALF)], split, ((1,), (0,)))
        wait_rows(step, error, error_rows, sems)
        total[...] += dot(split, error_rows[step], ((0,), (0,)))

    halves(core, error.shape[0], HALF, body, own, other)
    hidden_copy.wait()
    spread = pair(folded(tokens_sum[...]))
    turned = total[...] + dot(spread, hidden_in[...], ((0,), (0,)))
    total[:rank, :] = turned[:rank, :] + turned[rank:, :]
    half = mine.shape[0]
    mine[...] = total[:rank, pl.ds(pl.multiple_of(core * half, half), half)].T
    theirs[...] = total[:rank, pl.ds(pl.multiple_of((1 - core) * half, half), half)].T
    gram[...] = folded(gram_sum[:rank, :] + gram_sum[rank:, :])

def query_part(acts, hidden, error, own, other):
    tokens, rows = acts.shape
    columns = hidden.shape[1]
    rank = own.shape[1]
    half = (columns // CORES, rank)
    return pl.pallas_call(
        query_kernel,
        grid=(1,),
        in_specs=[HBM, HBM, HBM, whole(own.shape), whole(own.shape)],
        out_specs=(whole(half), whole(half), whole((rank, rank))),
        out_shape=(
            jax.ShapeDtypeStruct(half, F32),
            jax.ShapeDtypeStruct(half, F32),
            jax.ShapeDtypeStruct((rank, rank), F32),
        ),
        scratch_shapes=[
            pltpu.VMEM((tokens, rows), BF16),
            pltpu.VMEM((tokens, columns), BF16),
            pltpu.VMEM((rows // HALF, HALF, columns), BF16),
            pltpu.VMEM((2 * rank, columns), F32),
            pltpu.VMEM((tokens, 2 * rank), F32),
            pltpu.VMEM((2 * rank, 2 * rank), F32),
            pltpu.SemaphoreType.DMA((2,)),
            pltpu.SemaphoreType.DMA((rows // HALF,)),
        ],
        compiler_params=pltpu.CompilerParams(vmem_limit_bytes=VMEM_LIMIT),
        cost_estimate=pl.CostEstimate(
            flops=4 * rows * columns * rank, bytes_accessed=2 * rows * columns, transcendentals=0
        ),
        name="query_part",
    )(acts, hidden, error, own, other)

def triple(x):
    split = pair(x)
    return jnp.concatenate([split, split[:, : x.shape[1]]], axis=1)

def stacked(x):
    high = x.astype(BF16)
    rest = (x - high.astype(F32)).astype(BF16)
    return jnp.concatenate([high, high, rest], axis=0)

def residual_kernel(acts, hidden, error, own, other, inverse, query_own, query_other,
                    out, update, query,
                    acts_in, hidden_in, error_rows, turn, factors, small, sems, sent):
    replica = lax.axis_index("dp")
    core = lax.rem(replica, CORES)
    rank = inverse.shape[0]
    rows = error.shape[0]
    acts_copy = load(acts, acts_in, small.at[0])
    hidden_copy = load(hidden, hidden_in, small.at[1])
    start_rows(core, error, error_rows, sems)
    turn[...] = stacked(inverse[...])
    scale = 1.0 / lax.axis_size("dp")
    half = query_own.shape[0]
    for ref, first in ((query_own, core * half), (query_other, (1 - core) * half)):
        query[pl.ds(pl.multiple_of(first, half), half), :] = (
            dot(triple(ref[...]), turn[...], ((1,), (0,))) * scale
        )
    factors[: 3 * rank, :] = stacked(query[...].T)
    hidden_copy.wait()
    factors[3 * rank :, :] = -hidden_in[...]
    share = update.shape[0]
    first = replica * share
    within = lax.rem(first, rows // CORES)
    at = pl.ds(pl.multiple_of(within, 8), share)
    own_half = jnp.where(first < rows // CORES, 0, 1) == core
    picked = jnp.where(own_half, own[at, :], other[at, :])
    basis = dot(triple(picked), turn[...], ((1,), (0,)))
    update[...] = dot(triple(basis), factors[: 3 * rank, :], ((1,), (0,)))
    acts_copy.wait()

    def body(step, row, at, ref):
        basis = dot(triple(ref[pl.ds(at, BLOCK), :]), turn[...], ((1,), (0,)))
        mixed = jnp.concatenate([triple(basis), acts_in[:, pl.ds(row, BLOCK)].T], axis=1)
        change = dot(mixed, factors[...], ((1,), (0,)))
        wait_rows(step, error, error_rows, sems)
        error_rows[step] = (error_rows[step].astype(F32) - change).astype(BF16)
        load(error_rows.at[step], out.at[pl.ds(row, BLOCK)], sent.at[step])

    halves(core, rows, BLOCK, body, own, other)

    def drain(step, carry):
        pltpu.make_async_copy(error_rows.at[step], out.at[pl.ds(0, BLOCK)], sent.at[step]).wait()
        return carry

    lax.fori_loop(0, rows // BLOCK, drain, 0)

def residual(acts, hidden, error, own, other, inverse, query_own, query_other, share):
    tokens, rows = acts.shape
    columns = hidden.shape[1]
    rank = inverse.shape[0]
    return pl.pallas_call(
        residual_kernel,
        grid=(1,),
        in_specs=[
            HBM, HBM, HBM, whole(own.shape), whole(own.shape), whole(inverse.shape),
            whole(query_own.shape), whole(query_own.shape),
        ],
        out_specs=(HBM, whole((share, columns)), whole((columns, rank))),
        out_shape=(
            jax.ShapeDtypeStruct((rows, columns), BF16),
            jax.ShapeDtypeStruct((share, columns), F32),
            jax.ShapeDtypeStruct((columns, rank), F32),
        ),
        scratch_shapes=[
            pltpu.VMEM((tokens, rows), BF16),
            pltpu.VMEM((tokens, columns), BF16),
            pltpu.VMEM((rows // BLOCK, BLOCK, columns), BF16),
            pltpu.VMEM((3 * rank, rank), BF16),
            pltpu.VMEM((3 * rank + tokens, columns), BF16),
            pltpu.SemaphoreType.DMA((2,)),
            pltpu.SemaphoreType.DMA((rows // BLOCK,)),
            pltpu.SemaphoreType.DMA((rows // BLOCK,)),
        ],
        compiler_params=pltpu.CompilerParams(vmem_limit_bytes=VMEM_LIMIT),
        cost_estimate=pl.CostEstimate(
            flops=8 * rows * columns * rank, bytes_accessed=4 * rows * columns, transcendentals=0
        ),
        name="residual",
    )(acts, hidden, error, own, other, inverse, query_own, query_other)


def chips_of(replicas):
    return [list(range(core, replicas, CORES)) for core in range(CORES)]

def swapped(x, replicas):
    return lax.ppermute(x, "dp", [(i, i ^ 1) for i in range(replicas)])

def scatter_sum(x, replicas):
    chips = replicas // CORES
    pieces = lax.all_to_all(
        x.reshape(chips, x.shape[0] // chips, -1), "dp", 0, 0, axis_index_groups=chips_of(replicas)
    )
    return jnp.sum(pieces, axis=0)


def gather_rows(x, replicas):
    chips = replicas // CORES
    spread = jnp.broadcast_to(x[None], (chips, *x.shape))
    mine = lax.all_to_all(spread, "dp", 0, 0, axis_index_groups=chips_of(replicas))
    return mine.reshape(chips * x.shape[0], -1)

def sum_over_mp(x):
    ranks = lax.axis_size("mp")
    spread = jnp.broadcast_to(x[None], (ranks, *x.shape))
    return jnp.sum(lax.all_to_all(spread, "mp", 0, 0), axis=0)

SUB = 32
GROUP = 8

def inverse_factor_kernel(gram, out, table):
    rank = gram.shape[0]
    table[:, :rank] = gram[...]
    row = lax.broadcasted_iota(jnp.int32, (rank, rank), 0)
    column = lax.broadcasted_iota(jnp.int32, (rank, rank), 1)
    table[:, rank:] = jnp.where(row == column, 1.0, 0.0)
    shape = (SUB, rank)
    place = lax.broadcasted_iota(jnp.int32, shape, 0)
    for first in range(0, rank, SUB):
        parts = [table[first : first + SUB, :rank], table[first : first + SUB, rank:]]
        for j in range(SUB):
            if j % GROUP == 0:
                columns = [
                    jnp.broadcast_to(parts[0][:, first + k : first + k + 1], shape)
                    for k in range(j, j + GROUP)
                ]
            across = columns.pop(0)
            pivot = across[j : j + 1, :]
            scale = lax.rsqrt(pivot)
            factor = jnp.where(place > j, across * (scale * scale), 0.0)
            columns = [x - factor * x[j : j + 1, :] for x in columns]
            keep = jnp.where(place == j, scale, 1.0)
            parts = [x * keep - factor * x[j : j + 1, :] for x in parts]
        panel = jnp.concatenate(parts, axis=1)
        table[first : first + SUB, :] = panel
        if first + SUB < rank:
            change = lax.dot_general(
                parts[0],
                panel,
                (((0,), (0,)), ((), ())),
                precision=HIGHEST,
                preferred_element_type=F32,
            )
            table[first + SUB :, :] -= change[first + SUB :, :]
    out[...] = table[:, rank:].T

def inverse_factor(gram_matrix):
    rank = gram_matrix.shape[0]
    return pl.pallas_call(
        inverse_factor_kernel,
        out_shape=jax.ShapeDtypeStruct((rank, rank), F32),
        grid=(1,),
        in_specs=[pl.BlockSpec((rank, rank), lambda i: (0, 0))],
        out_specs=pl.BlockSpec((rank, rank), lambda i: (0, 0)),
        scratch_shapes=[pltpu.VMEM((rank, 2 * rank), F32)],
        compiler_params=pltpu.CompilerParams(vmem_limit_bytes=VMEM_LIMIT),
        cost_estimate=pl.CostEstimate(flops=2 * 10**9, bytes_accessed=10**7, transcendentals=128),
        name="inverse_factor",
    )(gram_matrix)

def after(x, earlier):
    return lax.optimization_barrier((x, earlier))[0]


def local(activations, grad_hidden, up_weight, error_feedback, query_previous):
    replicas = lax.axis_size("dp")
    error = error_feedback[0]
    mine, theirs = project_part(activations, grad_hidden, error, query_previous)
    mine = mine + swapped(theirs, replicas)
    own = gather_rows(sum_over_mp(scatter_sum(mine, replicas)), replicas)
    other = swapped(own, replicas)
    mine, theirs, gram_matrix = query_part(activations, grad_hidden, error, own, other)
    inverse = inverse_factor(gram_matrix)
    weight = lax.all_gather(up_weight, "dp", axis=0, tiled=True)
    partial_input = dot(after(grad_hidden, gram_matrix), weight, ((1,), (1,)))
    mine = after(mine + swapped(theirs, replicas), partial_input[0, 0])
    grad_input = lax.psum_scatter(partial_input, "mp", scatter_dimension=1, tiled=True)
    query_own = gather_rows(scatter_sum(mine, replicas), replicas)
    query_own, inverse = lax.optimization_barrier((query_own, inverse))
    query_other = swapped(query_own, replicas)
    error_next, update, query_next = residual(
        activations, grad_hidden, error, own, other, inverse, query_own, query_other,
        error.shape[0] // replicas,
    )
    grad_input, error_next = lax.optimization_barrier((grad_input, error_next))
    return (grad_input.astype(BF16), error_next[None], update, query_next)

def solution(mesh):
    in_specs = (P("dp", None), P("dp", "mp"), P("dp", "mp"), P("dp", None, "mp"), P("mp", None))
    out_specs = (P("dp", "mp"), P("dp", None, "mp"), P("dp", "mp"), P("mp", None))
    return jax.shard_map(local, mesh=mesh, in_specs=in_specs, out_specs=out_specs, check_vma=False)
```

```python
import functools

import jax
import jax.numpy as jnp
from jax import lax
from jax.experimental import pallas as pl
from jax.experimental.pallas import tpu as pltpu
from jax.sharding import PartitionSpec as P

HIGHEST = lax.Precision.HIGHEST
F32 = jnp.float32
BF16 = jnp.bfloat16
BLOCK = 640
HALF = 1280
CORES = 2
VMEM_LIMIT = 48 << 20

def dot(a, b, dims):
    return lax.dot_general(a, b, (dims, ((), ())), preferred_element_type=F32)

def pair(x):
    high = x.astype(BF16)
    rest = (x - high.astype(F32)).astype(BF16)
    return jnp.concatenate([high, rest], axis=1)

def folded(x):
    half = x.shape[1] // 2
    return x[:, :half] + x[:, half:]

def load(source, target, sem):
    copy = pltpu.make_async_copy(source, target, sem)
    copy.start()
    return copy

def row_of(step, core, rows, block):
    half = rows // CORES
    steps = half // block
    own = jnp.where(step < steps, core, 1 - core)
    return pl.multiple_of(own * half + lax.rem(step, steps) * block, block)

def start_rows(core, error, error_rows, sems):
    rows, (steps, block, _) = error.shape[0], error_rows.shape

    def start(step, carry):
        load(error.at[pl.ds(row_of(step, core, rows, block), block)], error_rows.at[step], sems.at[step])
        return carry

    lax.fori_loop(0, steps, start, 0)

def wait_rows(step, error, error_rows, sems):
    pltpu.make_async_copy(error.at[pl.ds(0, error_rows.shape[1])], error_rows.at[step], sems.at[step]).wait()

def halves(core, rows, block, body, first, second):
    steps = rows // CORES // block
    for base, ref in ((0, first), (steps, second)):

        def step_of(i, carry, base=base, ref=ref):
            body(base + i, row_of(base + i, core, rows, block), pl.multiple_of(i * block, block), ref)
            return carry

        lax.fori_loop(0, steps, step_of, 0)

def project_kernel(acts, hidden, error, query, mine, theirs,
                   acts_in, hidden_in, query_in, error_rows, query_pair, token_pair, small, sems):
    core = lax.rem(lax.axis_index("dp"), CORES)
    copies = [
        load(query, query_in, small.at[0]),
        load(hidden, hidden_in, small.at[1]),
        load(acts, acts_in, small.at[2]),
    ]
    start_rows(core, error, error_rows, sems)
    copies[0].wait()
    split = pair(query_in[...])
    query_pair[...] = split
    copies[1].wait()
    token_pair[...] = pair(folded(dot(hidden_in[...], split, ((1,), (0,)))))
    copies[2].wait()

    def body(step, row, at, ref):
        wait_rows(step, error, error_rows, sems)
        total = dot(error_rows[step], query_pair[...], ((1,), (0,)))
        total += dot(acts_in[:, pl.ds(row, BLOCK)], token_pair[...], ((0,), (0,)))
        ref[pl.ds(at, BLOCK), :] = folded(total)

    halves(core, error.shape[0], BLOCK, body, mine, theirs)

HBM = pl.BlockSpec(memory_space=pltpu.HBM)

def whole(shape):
    return pl.BlockSpec(shape, lambda i: (0,) * len(shape))

def project_part(acts, hidden, error, query):
    tokens, rows = acts.shape
    columns, rank = query.shape
    half = (rows // CORES, rank)
    return pl.pallas_call(
        project_kernel,
        grid=(1,),
        in_specs=[HBM, HBM, HBM, HBM],
        out_specs=(whole(half), whole(half)),
        out_shape=(jax.ShapeDtypeStruct(half, F32),) * 2,
        scratch_shapes=[
            pltpu.VMEM((tokens, rows), BF16),
            pltpu.VMEM((tokens, columns), BF16),
            pltpu.VMEM((columns, rank), F32),
            pltpu.VMEM((rows // BLOCK, BLOCK, columns), BF16),
            pltpu.VMEM((columns, 2 * rank), BF16),
            pltpu.VMEM((tokens, 2 * rank), BF16),
            pltpu.SemaphoreType.DMA((3,)),
            pltpu.SemaphoreType.DMA((rows // BLOCK,)),
        ],
        compiler_params=pltpu.CompilerParams(vmem_limit_bytes=60 << 20),
        cost_estimate=pl.CostEstimate(
            flops=4 * rows * columns * rank, bytes_accessed=2 * rows * columns, transcendentals=0
        ),
        name="project_part",
    )(acts, hidden, error, query)

def query_kernel(acts, hidden, error, own, other, mine, theirs, gram,
                 acts_in, hidden_in, error_rows, total, tokens_sum, gram_sum, small, sems):
    core = lax.rem(lax.axis_index("dp"), CORES)
    rank = gram.shape[0]
    acts_copy = load(acts, acts_in, small.at[0])
    start_rows(core, error, error_rows, sems)
    hidden_copy = load(hidden, hidden_in, small.at[1])
    total[...] = jnp.zeros_like(total)
    tokens_sum[...] = jnp.zeros_like(tokens_sum)
    gram_sum[...] = jnp.zeros_like(gram_sum)
    acts_copy.wait()

    def body(step, row, at, ref):
        split = pair(ref[pl.ds(at, HALF), :])
        gram_sum[...] += dot(split, split, ((0,), (0,)))
        tokens_sum[...] += dot(acts_in[:, pl.ds(row, HALF)], split, ((1,), (0,)))
        wait_rows(step, error, error_rows, sems)
        total[...] += dot(split, error_rows[step], ((0,), (0,)))

    halves(core, error.shape[0], HALF, body, own, other)
    hidden_copy.wait()
    spread = pair(folded(tokens_sum[...]))
    turned = total[...] + dot(spread, hidden_in[...], ((0,), (0,)))
    total[:rank, :] = turned[:rank, :] + turned[rank:, :]
    half = mine.shape[0]
    mine[...] = total[:rank, pl.ds(pl.multiple_of(core * half, half), half)].T
    theirs[...] = total[:rank, pl.ds(pl.multiple_of((1 - core) * half, half), half)].T
    gram[...] = folded(gram_sum[:rank, :] + gram_sum[rank:, :])

def query_part(acts, hidden, error, own, other):
    tokens, rows = acts.shape
    columns = hidden.shape[1]
    rank = own.shape[1]
    half = (columns // CORES, rank)
    return pl.pallas_call(
        query_kernel,
        grid=(1,),
        in_specs=[HBM, HBM, HBM, whole(own.shape), whole(own.shape)],
        out_specs=(whole(half), whole(half), whole((rank, rank))),
        out_shape=(
            jax.ShapeDtypeStruct(half, F32),
            jax.ShapeDtypeStruct(half, F32),
            jax.ShapeDtypeStruct((rank, rank), F32),
        ),
        scratch_shapes=[
            pltpu.VMEM((tokens, rows), BF16),
            pltpu.VMEM((tokens, columns), BF16),
            pltpu.VMEM((rows // HALF, HALF, columns), BF16),
            pltpu.VMEM((2 * rank, columns), F32),
            pltpu.VMEM((tokens, 2 * rank), F32),
            pltpu.VMEM((2 * rank, 2 * rank), F32),
            pltpu.SemaphoreType.DMA((2,)),
            pltpu.SemaphoreType.DMA((rows // HALF,)),
        ],
        compiler_params=pltpu.CompilerParams(vmem_limit_bytes=VMEM_LIMIT),
        cost_estimate=pl.CostEstimate(
            flops=4 * rows * columns * rank, bytes_accessed=2 * rows * columns, transcendentals=0
        ),
        name="query_part",
    )(acts, hidden, error, own, other)

def triple(x):
    split = pair(x)
    return jnp.concatenate([split, split[:, : x.shape[1]]], axis=1)

def stacked(x):
    high = x.astype(BF16)
    rest = (x - high.astype(F32)).astype(BF16)
    return jnp.concatenate([high, high, rest], axis=0)

def residual_kernel(acts, hidden, error, own, other, inverse, query_own, query_other,
                    out, update, query,
                    acts_in, hidden_in, error_rows, turn, factors, small, sems, sent):
    replica = lax.axis_index("dp")
    core = lax.rem(replica, CORES)
    rank = inverse.shape[0]
    rows = error.shape[0]
    acts_copy = load(acts, acts_in, small.at[0])
    hidden_copy = load(hidden, hidden_in, small.at[1])
    start_rows(core, error, error_rows, sems)
    turn[...] = stacked(inverse[...])
    scale = 1.0 / lax.axis_size("dp")
    half = query_own.shape[0]
    for ref, first in ((query_own, core * half), (query_other, (1 - core) * half)):
        query[pl.ds(pl.multiple_of(first, half), half), :] = (
            dot(triple(ref[...]), turn[...], ((1,), (0,))) * scale
        )
    factors[: 3 * rank, :] = stacked(query[...].T)
    hidden_copy.wait()
    factors[3 * rank :, :] = -hidden_in[...]
    share = update.shape[0]
    first = replica * share
    within = lax.rem(first, rows // CORES)
    at = pl.ds(pl.multiple_of(within, 8), share)
    own_half = jnp.where(first < rows // CORES, 0, 1) == core
    picked = jnp.where(own_half, own[at, :], other[at, :])
    basis = dot(triple(picked), turn[...], ((1,), (0,)))
    update[...] = dot(triple(basis), factors[: 3 * rank, :], ((1,), (0,)))
    acts_copy.wait()

    def body(step, row, at, ref):
        basis = dot(triple(ref[pl.ds(at, BLOCK), :]), turn[...], ((1,), (0,)))
        mixed = jnp.concatenate([triple(basis), acts_in[:, pl.ds(row, BLOCK)].T], axis=1)
        change = dot(mixed, factors[...], ((1,), (0,)))
        wait_rows(step, error, error_rows, sems)
        error_rows[step] = (error_rows[step].astype(F32) - change).astype(BF16)
        load(error_rows.at[step], out.at[pl.ds(row, BLOCK)], sent.at[step])

    halves(core, rows, BLOCK, body, own, other)

    def drain(step, carry):
        pltpu.make_async_copy(error_rows.at[step], out.at[pl.ds(0, BLOCK)], sent.at[step]).wait()
        return carry

    lax.fori_loop(0, rows // BLOCK, drain, 0)

def residual(acts, hidden, error, own, other, inverse, query_own, query_other, share):
    tokens, rows = acts.shape
    columns = hidden.shape[1]
    rank = inverse.shape[0]
    return pl.pallas_call(
        residual_kernel,
        grid=(1,),
        in_specs=[
            HBM, HBM, HBM, whole(own.shape), whole(own.shape), whole(inverse.shape),
            whole(query_own.shape), whole(query_own.shape),
        ],
        out_specs=(HBM, whole((share, columns)), whole((columns, rank))),
        out_shape=(
            jax.ShapeDtypeStruct((rows, columns), BF16),
            jax.ShapeDtypeStruct((share, columns), F32),
            jax.ShapeDtypeStruct((columns, rank), F32),
        ),
        scratch_shapes=[
            pltpu.VMEM((tokens, rows), BF16),
            pltpu.VMEM((tokens, columns), BF16),
            pltpu.VMEM((rows // BLOCK, BLOCK, columns), BF16),
            pltpu.VMEM((3 * rank, rank), BF16),
            pltpu.VMEM((3 * rank + tokens, columns), BF16),
            pltpu.SemaphoreType.DMA((2,)),
            pltpu.SemaphoreType.DMA((rows // BLOCK,)),
            pltpu.SemaphoreType.DMA((rows // BLOCK,)),
        ],
        compiler_params=pltpu.CompilerParams(vmem_limit_bytes=VMEM_LIMIT),
        cost_estimate=pl.CostEstimate(
            flops=8 * rows * columns * rank, bytes_accessed=4 * rows * columns, transcendentals=0
        ),
        name="residual",
    )(acts, hidden, error, own, other, inverse, query_own, query_other)


def chips_of(replicas):
    return [list(range(core, replicas, CORES)) for core in range(CORES)]

def swapped(x, replicas):
    return lax.ppermute(x, "dp", [(i, i ^ 1) for i in range(replicas)])

def scatter_sum(x, replicas):
    chips = replicas // CORES
    pieces = lax.all_to_all(
        x.reshape(chips, x.shape[0] // chips, -1), "dp", 0, 0, axis_index_groups=chips_of(replicas)
    )
    return jnp.sum(pieces, axis=0)


def gather_rows(x, replicas):
    chips = replicas // CORES
    spread = jnp.broadcast_to(x[None], (chips, *x.shape))
    mine = lax.all_to_all(spread, "dp", 0, 0, axis_index_groups=chips_of(replicas))
    return mine.reshape(chips * x.shape[0], -1)

def sum_over_mp(x):
    ranks = lax.axis_size("mp")
    spread = jnp.broadcast_to(x[None], (ranks, *x.shape))
    return jnp.sum(lax.all_to_all(spread, "mp", 0, 0), axis=0)

SUB = 32
GROUP = 8

def inverse_factor_kernel(gram, out, table):
    rank = gram.shape[0]
    table[:, :rank] = gram[...]
    row = lax.broadcasted_iota(jnp.int32, (rank, rank), 0)
    column = lax.broadcasted_iota(jnp.int32, (rank, rank), 1)
    table[:, rank:] = jnp.where(row == column, 1.0, 0.0)
    shape = (SUB, rank)
    place = lax.broadcasted_iota(jnp.int32, shape, 0)
    for first in range(0, rank, SUB):
        parts = [table[first : first + SUB, :rank], table[first : first + SUB, rank:]]
        for j in range(SUB):
            if j % GROUP == 0:
                columns = [
                    jnp.broadcast_to(parts[0][:, first + k : first + k + 1], shape)
                    for k in range(j, j + GROUP)
                ]
            across = columns.pop(0)
            pivot = across[j : j + 1, :]
            scale = lax.rsqrt(pivot)
            factor = jnp.where(place > j, across * (scale * scale), 0.0)
            columns = [x - factor * x[j : j + 1, :] for x in columns]
            keep = jnp.where(place == j, scale, 1.0)
            parts = [x * keep - factor * x[j : j + 1, :] for x in parts]
        panel = jnp.concatenate(parts, axis=1)
        table[first : first + SUB, :] = panel
        if first + SUB < rank:
            change = lax.dot_general(
                parts[0],
                panel,
                (((0,), (0,)), ((), ())),
                precision=HIGHEST,
                preferred_element_type=F32,
            )
            table[first + SUB :, :] -= change[first + SUB :, :]
    out[...] = table[:, rank:].T

def inverse_factor(gram_matrix):
    rank = gram_matrix.shape[0]
    return pl.pallas_call(
        inverse_factor_kernel,
        out_shape=jax.ShapeDtypeStruct((rank, rank), F32),
        grid=(1,),
        in_specs=[pl.BlockSpec((rank, rank), lambda i: (0, 0))],
        out_specs=pl.BlockSpec((rank, rank), lambda i: (0, 0)),
        scratch_shapes=[pltpu.VMEM((rank, 2 * rank), F32)],
        compiler_params=pltpu.CompilerParams(vmem_limit_bytes=VMEM_LIMIT),
        cost_estimate=pl.CostEstimate(flops=2 * 10**9, bytes_accessed=10**7, transcendentals=128),
        name="inverse_factor",
    )(gram_matrix)

def product_kernel(weight, hidden, out):
    out[...] = dot(weight[...], hidden[...], ((1,), (1,)))


def product(weight, hidden):
    rows, columns = weight.shape
    tokens = hidden.shape[0]
    return pl.pallas_call(
        product_kernel,
        grid=(rows // BLOCK,),
        in_specs=[
            pl.BlockSpec((BLOCK, columns), lambda i: (i, 0)),
            pl.BlockSpec((tokens, columns), lambda i: (0, 0)),
        ],
        out_specs=pl.BlockSpec((BLOCK, tokens), lambda i: (i, 0)),
        out_shape=jax.ShapeDtypeStruct((rows, tokens), F32),
        compiler_params=pltpu.CompilerParams(vmem_limit_bytes=VMEM_LIMIT),
        cost_estimate=pl.CostEstimate(
            flops=2 * rows * columns * tokens, bytes_accessed=2 * rows * columns, transcendentals=0
        ),
        name="product",
    )(weight, hidden)


def after(x, earlier):
    return lax.optimization_barrier((x, earlier))[0]


def local(activations, grad_hidden, up_weight, error_feedback, query_previous):
    replicas = lax.axis_size("dp")
    error = error_feedback[0]
    mine, theirs = project_part(activations, grad_hidden, error, query_previous)
    mine = mine + swapped(theirs, replicas)
    own = gather_rows(sum_over_mp(scatter_sum(mine, replicas)), replicas)
    other = swapped(own, replicas)
    mine, theirs, gram_matrix = query_part(activations, grad_hidden, error, own, other)
    inverse = inverse_factor(gram_matrix)
    weight = lax.all_gather(up_weight, "dp", axis=0, tiled=True)
    partial_input = product(weight, after(grad_hidden, gram_matrix))
    mine = after(mine + swapped(theirs, replicas), partial_input[0, 0])
    grad_input = lax.psum_scatter(partial_input, "mp", scatter_dimension=0, tiled=True)
    query_own = gather_rows(scatter_sum(mine, replicas), replicas)
    query_own, inverse = lax.optimization_barrier((query_own, inverse))
    query_other = swapped(query_own, replicas)
    error_next, update, query_next = residual(
        activations, grad_hidden, error, own, other, inverse, query_own, query_other,
        error.shape[0] // replicas,
    )
    grad_input, error_next = lax.optimization_barrier((grad_input, error_next))
    return (grad_input.astype(BF16).T, error_next[None], update, query_next)

def solution(mesh):
    in_specs = (P("dp", None), P("dp", "mp"), P("dp", "mp"), P("dp", None, "mp"), P("mp", None))
    out_specs = (P("dp", "mp"), P("dp", None, "mp"), P("dp", "mp"), P("mp", None))
    return jax.shard_map(local, mesh=mesh, in_specs=in_specs, out_specs=out_specs, check_vma=False)
```

```python
import functools

import jax
import jax.numpy as jnp
from jax import lax
from jax.experimental import pallas as pl
from jax.experimental.pallas import tpu as pltpu
from jax.sharding import PartitionSpec as P

HIGHEST = lax.Precision.HIGHEST
F32 = jnp.float32
BF16 = jnp.bfloat16
BLOCK = 640
HALF = 1280
CORES = 2
VMEM_LIMIT = 48 << 20

def dot(a, b, dims):
    return lax.dot_general(a, b, (dims, ((), ())), preferred_element_type=F32)

def pair(x):
    high = x.astype(BF16)
    rest = (x - high.astype(F32)).astype(BF16)
    return jnp.concatenate([high, rest], axis=1)

def folded(x):
    half = x.shape[1] // 2
    return x[:, :half] + x[:, half:]

def load(source, target, sem):
    copy = pltpu.make_async_copy(source, target, sem)
    copy.start()
    return copy

def row_of(step, core, rows, block):
    half = rows // CORES
    steps = half // block
    own = jnp.where(step < steps, core, 1 - core)
    return pl.multiple_of(own * half + lax.rem(step, steps) * block, block)

def start_rows(core, error, error_rows, sems):
    rows, (steps, block, _) = error.shape[0], error_rows.shape

    def start(step, carry):
        load(error.at[pl.ds(row_of(step, core, rows, block), block)], error_rows.at[step], sems.at[step])
        return carry

    lax.fori_loop(0, steps, start, 0)

def wait_rows(step, error, error_rows, sems):
    pltpu.make_async_copy(error.at[pl.ds(0, error_rows.shape[1])], error_rows.at[step], sems.at[step]).wait()

def halves(core, rows, block, body, first, second):
    steps = rows // CORES // block
    for base, ref in ((0, first), (steps, second)):

        def step_of(i, carry, base=base, ref=ref):
            body(base + i, row_of(base + i, core, rows, block), pl.multiple_of(i * block, block), ref)
            return carry

        lax.fori_loop(0, steps, step_of, 0)

def project_kernel(acts, hidden, error, query, mine, theirs,
                   acts_in, hidden_in, query_in, error_rows, query_pair, token_pair, small, sems):
    core = lax.rem(lax.axis_index("dp"), CORES)
    copies = [
        load(query, query_in, small.at[0]),
        load(hidden, hidden_in, small.at[1]),
        load(acts, acts_in, small.at[2]),
    ]
    start_rows(core, error, error_rows, sems)
    copies[0].wait()
    split = pair(query_in[...])
    query_pair[...] = split
    copies[1].wait()
    token_pair[...] = pair(folded(dot(hidden_in[...], split, ((1,), (0,)))))
    copies[2].wait()

    def body(step, row, at, ref):
        wait_rows(step, error, error_rows, sems)
        total = dot(error_rows[step], query_pair[...], ((1,), (0,)))
        total += dot(acts_in[:, pl.ds(row, BLOCK)], token_pair[...], ((0,), (0,)))
        ref[pl.ds(at, BLOCK), :] = folded(total)

    halves(core, error.shape[0], BLOCK, body, mine, theirs)

HBM = pl.BlockSpec(memory_space=pltpu.HBM)

def whole(shape):
    return pl.BlockSpec(shape, lambda i: (0,) * len(shape))

def project_part(acts, hidden, error, query):
    tokens, rows = acts.shape
    columns, rank = query.shape
    half = (rows // CORES, rank)
    return pl.pallas_call(
        project_kernel,
        grid=(1,),
        in_specs=[HBM, HBM, HBM, HBM],
        out_specs=(whole(half), whole(half)),
        out_shape=(jax.ShapeDtypeStruct(half, F32),) * 2,
        scratch_shapes=[
            pltpu.VMEM((tokens, rows), BF16),
            pltpu.VMEM((tokens, columns), BF16),
            pltpu.VMEM((columns, rank), F32),
            pltpu.VMEM((rows // BLOCK, BLOCK, columns), BF16),
            pltpu.VMEM((columns, 2 * rank), BF16),
            pltpu.VMEM((tokens, 2 * rank), BF16),
            pltpu.SemaphoreType.DMA((3,)),
            pltpu.SemaphoreType.DMA((rows // BLOCK,)),
        ],
        compiler_params=pltpu.CompilerParams(vmem_limit_bytes=60 << 20),
        cost_estimate=pl.CostEstimate(
            flops=4 * rows * columns * rank, bytes_accessed=2 * rows * columns, transcendentals=0
        ),
        name="project_part",
    )(acts, hidden, error, query)

def query_kernel(acts, hidden, error, own, other, mine, theirs, gram,
                 acts_in, hidden_in, error_rows, total, tokens_sum, gram_sum, small, sems):
    core = lax.rem(lax.axis_index("dp"), CORES)
    rank = gram.shape[0]
    acts_copy = load(acts, acts_in, small.at[0])
    start_rows(core, error, error_rows, sems)
    hidden_copy = load(hidden, hidden_in, small.at[1])
    total[...] = jnp.zeros_like(total)
    tokens_sum[...] = jnp.zeros_like(tokens_sum)
    gram_sum[...] = jnp.zeros_like(gram_sum)
    acts_copy.wait()

    def body(step, row, at, ref):
        split = pair(ref[pl.ds(at, HALF), :])
        gram_sum[...] += dot(split, split, ((0,), (0,)))
        tokens_sum[...] += dot(acts_in[:, pl.ds(row, HALF)], split, ((1,), (0,)))
        wait_rows(step, error, error_rows, sems)
        total[...] += dot(split, error_rows[step], ((0,), (0,)))

    halves(core, error.shape[0], HALF, body, own, other)
    hidden_copy.wait()
    spread = pair(folded(tokens_sum[...]))
    turned = total[...] + dot(spread, hidden_in[...], ((0,), (0,)))
    total[:rank, :] = turned[:rank, :] + turned[rank:, :]
    half = mine.shape[0]
    mine[...] = total[:rank, pl.ds(pl.multiple_of(core * half, half), half)].T
    theirs[...] = total[:rank, pl.ds(pl.multiple_of((1 - core) * half, half), half)].T
    gram[...] = folded(gram_sum[:rank, :] + gram_sum[rank:, :])

def query_part(acts, hidden, error, own, other):
    tokens, rows = acts.shape
    columns = hidden.shape[1]
    rank = own.shape[1]
    half = (columns // CORES, rank)
    return pl.pallas_call(
        query_kernel,
        grid=(1,),
        in_specs=[HBM, HBM, HBM, whole(own.shape), whole(own.shape)],
        out_specs=(whole(half), whole(half), whole((rank, rank))),
        out_shape=(
            jax.ShapeDtypeStruct(half, F32),
            jax.ShapeDtypeStruct(half, F32),
            jax.ShapeDtypeStruct((rank, rank), F32),
        ),
        scratch_shapes=[
            pltpu.VMEM((tokens, rows), BF16),
            pltpu.VMEM((tokens, columns), BF16),
            pltpu.VMEM((rows // HALF, HALF, columns), BF16),
            pltpu.VMEM((2 * rank, columns), F32),
            pltpu.VMEM((tokens, 2 * rank), F32),
            pltpu.VMEM((2 * rank, 2 * rank), F32),
            pltpu.SemaphoreType.DMA((2,)),
            pltpu.SemaphoreType.DMA((rows // HALF,)),
        ],
        compiler_params=pltpu.CompilerParams(vmem_limit_bytes=VMEM_LIMIT),
        cost_estimate=pl.CostEstimate(
            flops=4 * rows * columns * rank, bytes_accessed=2 * rows * columns, transcendentals=0
        ),
        name="query_part",
    )(acts, hidden, error, own, other)

def triple(x):
    split = pair(x)
    return jnp.concatenate([split, split[:, : x.shape[1]]], axis=1)

def stacked(x):
    high = x.astype(BF16)
    rest = (x - high.astype(F32)).astype(BF16)
    return jnp.concatenate([high, high, rest], axis=0)

def residual_kernel(acts, hidden, error, own, other, inverse, query_own, query_other,
                    out, update, query,
                    acts_in, hidden_in, error_rows, turn, factors, small, sems, sent):
    replica = lax.axis_index("dp")
    core = lax.rem(replica, CORES)
    rank = inverse.shape[0]
    rows = error.shape[0]
    acts_copy = load(acts, acts_in, small.at[0])
    hidden_copy = load(hidden, hidden_in, small.at[1])
    start_rows(core, error, error_rows, sems)
    turn[...] = stacked(inverse[...])
    scale = 1.0 / lax.axis_size("dp")
    half = query_own.shape[0]
    for ref, first in ((query_own, core * half), (query_other, (1 - core) * half)):
        query[pl.ds(pl.multiple_of(first, half), half), :] = (
            dot(triple(ref[...]), turn[...], ((1,), (0,))) * scale
        )
    factors[: 3 * rank, :] = stacked(query[...].T)
    hidden_copy.wait()
    factors[3 * rank :, :] = -hidden_in[...]
    share = update.shape[0]
    first = replica * share
    within = lax.rem(first, rows // CORES)
    at = pl.ds(pl.multiple_of(within, 8), share)
    own_half = jnp.where(first < rows // CORES, 0, 1) == core
    picked = jnp.where(own_half, own[at, :], other[at, :])
    basis = dot(triple(picked), turn[...], ((1,), (0,)))
    update[...] = dot(triple(basis), factors[: 3 * rank, :], ((1,), (0,)))
    acts_copy.wait()

    def body(step, row, at, ref):
        basis = dot(triple(ref[pl.ds(at, BLOCK), :]), turn[...], ((1,), (0,)))
        mixed = jnp.concatenate([triple(basis), acts_in[:, pl.ds(row, BLOCK)].T], axis=1)
        change = dot(mixed, factors[...], ((1,), (0,)))
        wait_rows(step, error, error_rows, sems)
        error_rows[step] = (error_rows[step].astype(F32) - change).astype(BF16)
        load(error_rows.at[step], out.at[pl.ds(row, BLOCK)], sent.at[step])

    halves(core, rows, BLOCK, body, own, other)

    def drain(step, carry):
        pltpu.make_async_copy(error_rows.at[step], out.at[pl.ds(0, BLOCK)], sent.at[step]).wait()
        return carry

    lax.fori_loop(0, rows // BLOCK, drain, 0)

def residual(acts, hidden, error, own, other, inverse, query_own, query_other, share):
    tokens, rows = acts.shape
    columns = hidden.shape[1]
    rank = inverse.shape[0]
    return pl.pallas_call(
        residual_kernel,
        grid=(1,),
        in_specs=[
            HBM, HBM, HBM, whole(own.shape), whole(own.shape), whole(inverse.shape),
            whole(query_own.shape), whole(query_own.shape),
        ],
        out_specs=(HBM, whole((share, columns)), whole((columns, rank))),
        out_shape=(
            jax.ShapeDtypeStruct((rows, columns), BF16),
            jax.ShapeDtypeStruct((share, columns), F32),
            jax.ShapeDtypeStruct((columns, rank), F32),
        ),
        scratch_shapes=[
            pltpu.VMEM((tokens, rows), BF16),
            pltpu.VMEM((tokens, columns), BF16),
            pltpu.VMEM((rows // BLOCK, BLOCK, columns), BF16),
            pltpu.VMEM((3 * rank, rank), BF16),
            pltpu.VMEM((3 * rank + tokens, columns), BF16),
            pltpu.SemaphoreType.DMA((2,)),
            pltpu.SemaphoreType.DMA((rows // BLOCK,)),
            pltpu.SemaphoreType.DMA((rows // BLOCK,)),
        ],
        compiler_params=pltpu.CompilerParams(vmem_limit_bytes=VMEM_LIMIT),
        cost_estimate=pl.CostEstimate(
            flops=8 * rows * columns * rank, bytes_accessed=4 * rows * columns, transcendentals=0
        ),
        name="residual",
    )(acts, hidden, error, own, other, inverse, query_own, query_other)


def chips_of(replicas):
    return [list(range(core, replicas, CORES)) for core in range(CORES)]

def swapped(x, replicas):
    return lax.ppermute(x, "dp", [(i, i ^ 1) for i in range(replicas)])

def scatter_sum(x, replicas):
    chips = replicas // CORES
    pieces = lax.all_to_all(
        x.reshape(chips, x.shape[0] // chips, -1), "dp", 0, 0, axis_index_groups=chips_of(replicas)
    )
    return jnp.sum(pieces, axis=0)


def gather_rows(x, replicas):
    chips = replicas // CORES
    spread = jnp.broadcast_to(x[None], (chips, *x.shape))
    mine = lax.all_to_all(spread, "dp", 0, 0, axis_index_groups=chips_of(replicas))
    return mine.reshape(chips * x.shape[0], -1)

def sum_over_mp(x):
    ranks = lax.axis_size("mp")
    spread = jnp.broadcast_to(x[None], (ranks, *x.shape))
    return jnp.sum(lax.all_to_all(spread, "mp", 0, 0), axis=0)

SUB = 32
GROUP = 8

def inverse_factor_kernel(gram, out, table):
    rank = gram.shape[0]
    table[:, :rank] = gram[...]
    row = lax.broadcasted_iota(jnp.int32, (rank, rank), 0)
    column = lax.broadcasted_iota(jnp.int32, (rank, rank), 1)
    table[:, rank:] = jnp.where(row == column, 1.0, 0.0)
    shape = (SUB, rank)
    place = lax.broadcasted_iota(jnp.int32, shape, 0)
    for first in range(0, rank, SUB):
        parts = [table[first : first + SUB, :rank], table[first : first + SUB, rank:]]
        for j in range(SUB):
            if j % GROUP == 0:
                columns = [
                    jnp.broadcast_to(parts[0][:, first + k : first + k + 1], shape)
                    for k in range(j, j + GROUP)
                ]
            across = columns.pop(0)
            pivot = across[j : j + 1, :]
            scale = lax.rsqrt(pivot)
            factor = jnp.where(place > j, across * (scale * scale), 0.0)
            columns = [x - factor * x[j : j + 1, :] for x in columns]
            keep = jnp.where(place == j, scale, 1.0)
            parts = [x * keep - factor * x[j : j + 1, :] for x in parts]
        panel = jnp.concatenate(parts, axis=1)
        table[first : first + SUB, :] = panel
        if first + SUB < rank:
            change = lax.dot_general(
                parts[0],
                panel,
                (((0,), (0,)), ((), ())),
                precision=HIGHEST,
                preferred_element_type=F32,
            )
            table[first + SUB :, :] -= change[first + SUB :, :]
    out[...] = table[:, rank:].T

def inverse_factor(gram_matrix):
    rank = gram_matrix.shape[0]
    return pl.pallas_call(
        inverse_factor_kernel,
        out_shape=jax.ShapeDtypeStruct((rank, rank), F32),
        grid=(1,),
        in_specs=[pl.BlockSpec((rank, rank), lambda i: (0, 0))],
        out_specs=pl.BlockSpec((rank, rank), lambda i: (0, 0)),
        scratch_shapes=[pltpu.VMEM((rank, 2 * rank), F32)],
        compiler_params=pltpu.CompilerParams(vmem_limit_bytes=VMEM_LIMIT),
        cost_estimate=pl.CostEstimate(flops=2 * 10**9, bytes_accessed=10**7, transcendentals=128),
        name="inverse_factor",
    )(gram_matrix)

def after(x, earlier):
    return lax.optimization_barrier((x, earlier))[0]


def local(activations, grad_hidden, up_weight, error_feedback, query_previous):
    replicas = lax.axis_size("dp")
    error = error_feedback[0]
    mine, theirs = project_part(activations, grad_hidden, error, query_previous)
    mine = mine + swapped(theirs, replicas)
    own = gather_rows(sum_over_mp(scatter_sum(mine, replicas)), replicas)
    other = swapped(own, replicas)
    weight = lax.all_gather(up_weight, "dp", axis=0, tiled=True)
    partial_input = dot(grad_hidden, weight, ((1,), (1,)))
    grad_input = lax.psum_scatter(partial_input, "mp", scatter_dimension=1, tiled=True)
    mine, theirs, gram_matrix = query_part(activations, grad_hidden, error, own, other)
    inverse = inverse_factor(gram_matrix)
    mine = mine + swapped(theirs, replicas)
    query_own = gather_rows(scatter_sum(mine, replicas), replicas)
    query_own, inverse = lax.optimization_barrier((query_own, inverse))
    query_other = swapped(query_own, replicas)
    error_next, update, query_next = residual(
        activations, grad_hidden, error, own, other, inverse, query_own, query_other,
        error.shape[0] // replicas,
    )
    grad_input, error_next = lax.optimization_barrier((grad_input, error_next))
    return (grad_input.astype(BF16), error_next[None], update, query_next)

def solution(mesh):
    in_specs = (P("dp", None), P("dp", "mp"), P("dp", "mp"), P("dp", None, "mp"), P("mp", None))
    out_specs = (P("dp", "mp"), P("dp", None, "mp"), P("dp", "mp"), P("mp", None))
    return jax.shard_map(local, mesh=mesh, in_specs=in_specs, out_specs=out_specs, check_vma=False)
```
